512 devices in a mesh: section: 4 (over z_lo, core), cls: 128 (over z_hi, x, y).
Axes of the slice: x: 4, y: 8, z: 8 (z_hi: 4, z_lo: 2; z = z_hi * 2 + z_lo), core: 2. Of those that a mesh axis runs over, the one named last changes fastest.
Arguments:
- images: bfloat16 [8192, 256, 256], P(('section', 'cls')), may hold values from -6 to 6
- group_ids: int32 [8192], P(('section', 'cls')), may hold values from 0 to 3
- row_filters: bfloat16 [4, 256, 256], replicated, may hold values from -0.375 to 0.375
- column_filters: bfloat16 [4, 256, 256], replicated, may hold values from -0.375 to 0.375
- basis_rows: bfloat16 [256, 16], replicated, may hold values from -0.375 to 0.375
- basis_columns: bfloat16 [256, 16], replicated, may hold values from -0.375 to 0.375
- rotations: bfloat16 [36, 256, 256], P('section'), may hold values from -0.375 to 0.375
- references: bfloat16 [256, 256], P('cls'), may hold values from -2 to 2
- sharpness: bfloat16 [8192], P(('section', 'cls')), may hold values from 0.049804688 to 2
- best_rotation: int32 [8192], P(('section', 'cls')), may hold values from 0 to 35
- assignments: int32 [8192, 32], P(('section', 'cls')), may hold values from 0 to 255, all different within a row; in each aligned block of 16 rows (0 to 15, 16 to 31, ...) at most 2 rows name the same one
Outputs:
- new_references: float32 [256, 256], P('cls')
- evidence: float32 [8192], P(('section', 'cls'))
The draws below stay inside these ranges and needn't reach their ends.
Inputs may be any that keep to these rules, and one draw needn't show every extreme that they name: `assignments`: each particle lists 32 different classes; among the particles of one device no class is listed more than 2 times, a bound that some block reaches.
All inputs are finite; a program needn't handle non-finite values.
Results may differ from the reference program's by a relative error of at most 0.019.
Values may be sent and summed in bfloat16 or wider, within the bound.
A program may use at most 64 MiB of HBM per device.

```python
import math
import jax
import jax.numpy as jnp
import numpy as np
from jax import lax

PIX = 256
NB = 16
COEF = 256
ROT = 36
GROUPS = 4
PART_DEV = 16
CLASSES = 256
TOP = 32
PARTICLES = 8192
MOST = 2


def touch_ends(array, stream_key, low, top_value):
    longest = array.shape.index(max(array.shape))
    spots = []
    for shift in (0, 1):
        where = [jax.random.randint(jax.random.fold_in(stream_key, axis), (), 0, length) for axis, length in enumerate(array.shape)]
        where[longest] = (where[longest] + shift) % array.shape[longest]
        spots.append(tuple(where))
    return array.at[spots[0]].set(low).at[spots[1]].set(top_value)


def block_levels(own_key, dims, pieces, low, largest):
    loudness, own = 1.0, jax.random.fold_in(own_key, 6)
    for axis_at, parts in pieces:
        draws = jnp.exp(jax.random.uniform(jax.random.fold_in(own, axis_at), (parts,), jnp.float32, low / len(pieces), largest / len(pieces)))
        loudness = loudness * jnp.repeat(draws, dims[axis_at] // parts).reshape([-1 if axis == axis_at else 1 for axis in range(len(dims))])
    return loudness


def assign_block(stream_key, own, number, rows, number_of, top, bound, lean):
    sequence = jax.random.permutation(stream_key, number_of)
    crowded, ordinary = portions_of(number_of, rows * top, bound, lean, True), portions_of(number_of, rows * top, bound, lean, False)
    places = jnp.arange(number_of)

    def named(lengths, turn):
        used = int((lengths > 0).sum())
        fixed = max(1, used // 4)
        moved = fixed + (places - fixed + turn * (used - fixed)) % max(1, number_of - fixed)
        return jnp.zeros((number_of,), jnp.int32).at[sequence[jnp.where(places < fixed, places, moved)]].set(jnp.asarray(lengths, jnp.int32))

    lengths = jnp.where(number % 4 == 0, named(crowded, number // 4), named(ordinary, number - number // 4 - 1))
    mixed = jax.random.permutation(jax.random.fold_in(own, 3), number_of)
    source_of, sink = mixed[0:number_of // 2 * 2:2], mixed[1:number_of // 2 * 2:2]
    margin = jnp.minimum(lengths[source_of] - 1, bound - lengths[sink]) // 2
    margin = jnp.where((source_of == sequence[0]) | (sink == sequence[0]) | (lengths[sink] == 0), 0, jnp.maximum(margin, 0))
    moved = jax.random.randint(jax.random.fold_in(own, 4), (number_of // 2,), 0, 1 << 20) % (margin + 1)
    lengths = lengths.at[source_of].add(-moved).at[sink].add(moved)
    items = jnp.searchsorted(jnp.cumsum(lengths), jnp.arange(rows * top), side="right").astype(jnp.int32)
    grid = items.reshape(top, rows).T
    grid = grid[jax.random.permutation(jax.random.fold_in(own, 1), rows)]
    turn = jax.random.randint(jax.random.fold_in(own, 2), (rows, 1), 0, top)
    return jnp.take_along_axis(grid, (jnp.arange(top)[None, :] + turn) % top, axis=1)


def portions_of(amount, total, bound, slope, full):
    loads = [(1 << 20) // math.isqrt(rank ** slope) + 1 for rank in range(1, amount + 1)]
    largest = bound if full else min(bound, max(-(-total // amount), total * loads[0] // sum(loads)))
    least = 1 if total - largest >= amount - 1 else 0
    holding, surplus = [largest] + [least] * (amount - 1), total - largest - least * (amount - 1)
    while surplus > 0:
        candidates = [i for i in range(1, amount) if holding[i] < largest] or [i for i in range(1, amount) if holding[i] < bound]
        whole, left = sum([loads[i] for i in candidates]), surplus
        for i in candidates:
            extra = min(bound - holding[i], max(1, left * loads[i] // whole), surplus)
            holding[i] = holding[i] + extra
            surplus = surplus - extra
    return np.array(holding)


def noise(key, dims, scale, most, split=(), kind=jnp.bfloat16):
    array = scale * jax.random.normal(key, dims, jnp.float32)
    if split:
        array = array * block_levels(key, dims, split, -0.22, 0.18)
    return jnp.clip(array, -most, most).astype(kind)


def setup_inputs(seed: int = 0) -> dict:
    streams_of = jax.random.split(jax.random.key(seed), 12)
    images = noise(streams_of[0], (PARTICLES, PIX, PIX), 1.0, 6.0, ((0, 512),))
    group_ids = touch_ends(jax.random.randint(streams_of[1], (PARTICLES,), 0, GROUPS), jax.random.fold_in(streams_of[1], 1), 0, GROUPS - 1).astype(jnp.int32)
    row_filters = noise(streams_of[2], (GROUPS, PIX, PIX), PIX ** -0.5, 0.375)
    column_filters = noise(streams_of[3], (GROUPS, PIX, PIX), PIX ** -0.5, 0.375)
    basis_rows = noise(streams_of[4], (PIX, NB), PIX ** -0.5, 0.375)
    basis_columns = noise(streams_of[5], (PIX, NB), PIX ** -0.5, 0.375)
    rotations = noise(streams_of[6], (ROT, COEF, COEF), COEF ** -0.5, 0.375, ((0, 4),))
    references = noise(streams_of[7], (CLASSES, COEF), 0.125, 2.0, ((0, 128),))
    sharpness = jnp.clip(jnp.exp(math.log(2.0) - 3.6927934 * jax.random.uniform(streams_of[8], (PARTICLES,), jnp.float32) ** block_levels(streams_of[8], (PARTICLES,), ((0, 512),), -0.2, 0.2)), 0.049804688, 2.0).astype(jnp.bfloat16)
    best_rotation = touch_ends(jax.random.randint(streams_of[9], (PARTICLES,), 0, ROT), jax.random.fold_in(streams_of[9], 1), 0, ROT - 1).astype(jnp.int32)
    assignments_keys = jax.random.split(jax.random.fold_in(streams_of[10], 1), PARTICLES // PART_DEV)
    assignments_turns = jax.random.permutation(jax.random.fold_in(streams_of[10], 3), PARTICLES // PART_DEV)
    assignments = jax.vmap(lambda own, number: assign_block(jax.random.fold_in(streams_of[10], 2), own, number, PART_DEV, CLASSES, TOP, MOST, 2))(assignments_keys, assignments_turns).reshape((PARTICLES, TOP))
    return {"images": images, "group_ids": group_ids, "row_filters": row_filters, "column_filters": column_filters, "basis_rows": basis_rows, "basis_columns": basis_columns, "rotations": rotations, "references": references, "sharpness": sharpness, "best_rotation": best_rotation, "assignments": assignments}


EPSILON = 1e-05

def soft_edge(pixels):
    coordinate = (jnp.arange(pixels, dtype=jnp.float32) - (pixels - 1) / 2.0) / (pixels / 2.0)
    radius = jnp.sqrt(coordinate[:, None] * coordinate[:, None] + coordinate[None, :] * coordinate[None, :])
    falloff = jnp.clip((radius - 0.8) / 0.15, 0.0, 1.0)
    return 0.5 + 0.5 * jnp.cos(math.pi * falloff)

def filter_reference(block_images, block_groups, row_filters, column_filters, basis_rows, basis_columns):
    column_each = jnp.take(column_filters, block_groups, axis=0).astype(jnp.float32)
    row_each = jnp.take(row_filters, block_groups, axis=0).astype(jnp.float32)
    filtered_half = jnp.einsum('bij,bjk->bik', block_images.astype(jnp.float32), column_each).astype(jnp.bfloat16)
    filtered = jnp.einsum('bij,bjk->bik', row_each, filtered_half.astype(jnp.float32))
    masked = filtered * soft_edge(block_images.shape[1])
    power = lax.optimization_barrier(jnp.mean(masked * masked, axis=(1, 2), keepdims=True))
    normed = (masked * lax.rsqrt(power + EPSILON)).astype(jnp.bfloat16)
    inner = jnp.einsum('bij,jk->bik', normed.astype(jnp.float32), basis_columns.astype(jnp.float32))
    coeffs = jnp.einsum('ja,bjk->bak', basis_rows.astype(jnp.float32), inner, precision=lax.Precision.HIGHEST)
    return coeffs.reshape(coeffs.shape[0], -1).astype(jnp.bfloat16)

def reference(images, group_ids, row_filters, column_filters, basis_rows, basis_columns, rotations, references, sharpness, best_rotation, assignments):
    blocks = PARTICLES // PART_DEV

    def one_block(block_inputs):
        block_images, block_groups, block_sharpness, block_best, block_assign = block_inputs
        coeffs = filter_reference(block_images, block_groups, row_filters, column_filters, basis_rows, basis_columns)
        turned = jnp.einsum('rkl,nl->nrk', rotations.astype(jnp.float32), coeffs.astype(jnp.float32)).astype(jnp.bfloat16)
        scores = jnp.einsum('nrk,ck->nrc', turned.astype(jnp.float32), references.astype(jnp.float32))
        scores = scores * block_sharpness.astype(jnp.float32)[:, None, None]
        log_marg = jax.nn.logsumexp(scores, axis=1)
        evidence = jax.nn.logsumexp(log_marg, axis=1)
        matches = block_assign[:, :, None] == jnp.arange(CLASSES, dtype=jnp.int32)[None, None, :]
        picked = lax.optimization_barrier(jnp.sum(jnp.where(matches, log_marg[:, None, :], 0.0), axis=2))
        weights = jax.nn.softmax(picked, axis=1).astype(jnp.bfloat16)
        aligned = jnp.take_along_axis(turned, block_best.astype(jnp.int32)[:, None, None], axis=1)[:, 0, :]
        contribution = (weights.astype(jnp.float32)[:, :, None] * aligned.astype(jnp.float32)[:, None, :]).astype(jnp.bfloat16)
        return (evidence, contribution, weights)
    block_inputs = (images.reshape(blocks, PART_DEV, PIX, PIX), group_ids.reshape(blocks, PART_DEV), sharpness.reshape(blocks, PART_DEV), best_rotation.reshape(blocks, PART_DEV), assignments.reshape(blocks, PART_DEV, TOP))
    evidence, contribution, weights = lax.map(one_block, block_inputs)
    flat_classes = assignments.reshape(-1)
    class_sums = jax.ops.segment_sum(contribution.reshape(-1, COEF).astype(jnp.float32), flat_classes, num_segments=CLASSES)
    class_weights = jax.ops.segment_sum(weights.reshape(-1).astype(jnp.float32), flat_classes, num_segments=CLASSES)
    new_references = (class_sums + references.astype(jnp.float32)) / (class_weights[:, None] + 1.0)
    return (new_references, evidence.reshape(-1))
```

```python
import functools
import math

import jax
import jax.numpy as jnp
import numpy as np
from jax import lax
from jax.experimental import pallas as pl
from jax.experimental.pallas import tpu as pltpu
from jax.sharding import PartitionSpec as P

EPSILON = 1e-05
TORUS = (4, 4, 8)
MESH = pl.DeviceIdType.MESH
LANES = 128


def soft_edge(pixels):
    coordinate = (np.arange(pixels, dtype=np.float32) - np.float32((pixels - 1) / 2.0)) / np.float32(pixels / 2.0)
    radius = np.sqrt(coordinate[:, None] * coordinate[:, None] + coordinate[None, :] * coordinate[None, :])
    falloff = np.clip((radius - np.float32(0.8)) / np.float32(0.15), 0.0, 1.0)
    return (0.5 + 0.5 * np.cos(math.pi * falloff)).astype(np.float32)


def contract_last(a, b):
    return lax.dot_general(a, b, (((1,), (1,)), ((), ())), preferred_element_type=jnp.float32)


def contract_first(a, b):
    return lax.dot_general(a, b, (((0,), (0,)), ((), ())), preferred_element_type=jnp.float32)


def kernel(
    dims,
    images,
    group_ids,
    row_filters,
    column_filters,
    basis_rows,
    basis_columns,
    mask,
    rotations,
    references,
    sharpness,
    best_rotation,
    assignments,
    new_references,
    evidence,
    img,
    rowf,
    colf,
    edge,
    rot,
    bas,
    tiled,
    spread,
    raw,
    squares,
    near,
    refs,
    coef,
    turned_out,
    turned_in,
    marg_out,
    marg_in,
    sum_x,
    got_x,
    sum_y,
    got_y,
    sum_z,
    got_z,
    img_sem,
    in_sem,
    send_sem,
    recv_sem,
):
    nz, nx, ny = dims
    section, cls = lax.axis_index("section"), lax.axis_index("cls")
    sections = 4
    zh = cls // (nx * ny)
    xx = (cls // ny) % nx
    yy = cls % ny
    particles, pix = img.shape[0], img.shape[1]
    local = rot.shape[0]
    width = rot.shape[1]
    classes = nz * nx * ny * 2
    nb = bas.shape[1]

    def at(dz, dx, dy, ds):
        return {
            "section": (section + ds) % sections,
            "cls": (((zh + dz) % nz) * nx + (xx + dx) % nx) * ny + (yy + dy) % ny,
        }

    peers = [at(0, dx, 0, 0) for dx in range(1, nx)]
    peers += [at(0, 0, dy, 0) for dy in range(1, ny)]
    peers += [at(dz, 0, 0, ds) for dz in range(nz) for ds in range(sections) if (dz, ds) != (0, 0)]
    barrier = pltpu.get_barrier_semaphore()
    for peer in peers:
        pl.semaphore_signal(barrier, inc=1, device_id=peer, device_id_type=MESH)

    inputs = {}
    for k, (src, dst) in enumerate(
        [
            (column_filters, colf),
            (row_filters, rowf),
            (basis_rows, bas.at[0]),
            (basis_columns, bas.at[1]),
            (mask, edge),
            (rotations, rot),
        ]
    ):
        inputs[k] = pltpu.make_async_copy(src, dst, in_sem.at[k])
    for k in (2, 3, 0):
        inputs[k].start()
    pltpu.make_async_copy(images.at[0], img.at[0], img_sem.at[0]).start()
    for k in (1, 4):
        inputs[k].start()

    @pl.loop(1, particles)
    def _(n):
        pltpu.make_async_copy(images.at[n], img.at[n], img_sem.at[n]).start()

    inputs[5].start()

    inputs[2].wait()
    inputs[3].wait()
    row_at = lax.broadcasted_iota(jnp.int32, (nb, nb * nb), 0)
    lane_at = lax.broadcasted_iota(jnp.int32, (nb, nb * nb), 1)
    minor = (lane_at % nb == row_at).astype(jnp.float32).astype(jnp.bfloat16)
    major = (lane_at // nb == row_at).astype(jnp.float32).astype(jnp.bfloat16)
    tiled[...] = contract_first(bas[1], minor).astype(jnp.bfloat16)
    spread[...] = contract_first(bas[0], major)
    inputs[0].wait()
    inputs[1].wait()
    inputs[4].wait()

    def filter_image(n):
        pltpu.make_async_copy(images.at[n], img.at[n], img_sem.at[n]).wait()
        group = group_ids[n]
        half = jnp.dot(img[n], colf[group], preferred_element_type=jnp.float32).astype(jnp.bfloat16)
        masked = jnp.dot(rowf[group], half, preferred_element_type=jnp.float32) * edge[...]
        inner = jnp.dot(masked.astype(jnp.bfloat16), tiled[...], preferred_element_type=jnp.float32)
        squares[pl.ds(n, 1), :] = jnp.sum(masked * masked, axis=0, keepdims=True)
        raw[pl.ds(n, 1), :] = jnp.sum(inner * spread[...], axis=0, keepdims=True)

    def filter_images(low, high, together):
        @pl.loop(low, high, step=together)
        def _(n):
            for k in range(together):
                filter_image(n + k)

    def send(k, src, dst, to):
        pltpu.make_async_remote_copy(
            src_ref=src,
            dst_ref=dst,
            send_sem=send_sem.at[k],
            recv_sem=recv_sem.at[k],
            device_id=to,
            device_id_type=MESH,
        ).start()

    def arrived(k, ref):
        pltpu.make_async_copy(ref, ref, recv_sem.at[k]).wait()

    def sent(k, ref):
        pltpu.make_async_copy(ref, ref, send_sem.at[k]).wait()

    quarter = particles // 4
    filter_images(0, quarter, 2)

    pl.semaphore_wait(barrier, len(peers))
    near[0] = references[...].astype(jnp.float32).astype(jnp.bfloat16)
    for dz in range(1, nz):
        send(0, near.at[0], near.at[nz - dz], at(dz, 0, 0, 0))
    filter_images(quarter, 2 * quarter, 2)
    arrived(0, near.at[pl.ds(1, nz - 1)])
    refs[0, 0] = jnp.concatenate([near[dz].astype(jnp.float32) for dz in range(nz)], axis=0).astype(jnp.bfloat16)
    for dy in range(1, ny):
        send(1, refs.at[0, 0], refs.at[0, ny - dy], at(0, 0, dy, 0))
    filter_images(2 * quarter, 3 * quarter, 2)
    arrived(1, refs.at[0, pl.ds(1, ny - 1)])
    for dx in range(1, nx):
        send(2, refs.at[0], refs.at[nx - dx], at(0, dx, 0, 0))
    filter_images(3 * quarter, particles, 2)

    eye = lax.broadcasted_iota(jnp.int32, (particles, particles), 0) == lax.broadcasted_iota(
        jnp.int32, (particles, particles), 1
    )
    sharp_row = sharpness[...].astype(jnp.float32)
    sharp = jnp.sum(jnp.where(eye, jnp.broadcast_to(sharp_row, (particles, particles)), 0.0), axis=1, keepdims=True)
    best_row = best_rotation[...].astype(jnp.float32)
    best = jnp.sum(jnp.where(eye, jnp.broadcast_to(best_row, (particles, particles)), 0.0), axis=1, keepdims=True)
    power = jnp.sum(squares[...], axis=1, keepdims=True) * (1.0 / (pix * pix))
    scale = lax.rsqrt(power + EPSILON) * sharp
    coef[0, :, 0:width] = (raw[...] * scale).astype(jnp.bfloat16)
    coef[0, :, width:] = jnp.broadcast_to(best, (particles, LANES)).astype(jnp.bfloat16)
    for ds in range(1, sections):
        send(3, coef.at[0], coef.at[sections - ds], at(0, 0, 0, ds))

    place = lax.broadcasted_iota(jnp.int32, (particles, classes), 1)
    dx_at, rest = place // (ny * nz * 2), place % (ny * nz * 2)
    dy_at, rest = rest // (nz * 2), rest % (nz * 2)
    dz_at, last = rest // 2, rest % 2
    name = ((((zh + dz_at) % nz) * nx + (xx + dx_at) % nx) * ny + (yy + dy_at) % ny) * 2 + last
    listed = jnp.zeros((particles, classes), jnp.float32)
    for j in range(assignments.shape[1]):
        listed = jnp.where(assignments[:, j : j + 1] == name, 1.0, listed)

    inputs[5].wait()
    arrived(2, refs.at[pl.ds(1, nx - 1)])
    all_refs = refs[...].astype(jnp.float32).reshape(classes, width).astype(jnp.bfloat16)
    arrived(3, coef.at[pl.ds(1, sections - 1)])

    everyone = sections * particles
    gathered = coef[:, :, 0:width].reshape(everyone, width)
    best_all = coef[:, :, width:].astype(jnp.float32).reshape(everyone, LANES)
    best_all = jnp.concatenate([best_all] * (width // LANES), axis=1)
    first = (section * local).astype(jnp.float32)
    aligned = jnp.zeros((everyone, width), jnp.float32)
    turned = []
    for r in range(local):
        one = contract_last(gathered, rot[r])
        aligned = jnp.where(best_all == first + float(r), one, aligned)
        turned.append(one.astype(jnp.bfloat16))
    turned_out[...] = aligned.astype(jnp.bfloat16).reshape(sections, particles, width)
    for ds in range(1, sections):
        send(4, turned_out.at[ds], turned_in.at[sections - ds], at(0, 0, 0, ds))
    scores = [contract_last(one, all_refs) for one in turned]
    largest = functools.reduce(jnp.maximum, scores)
    total = functools.reduce(jnp.add, [jnp.exp(one - largest) for one in scores])
    marg_out[...] = (largest + jnp.log(total)).reshape(sections, particles, classes)
    for ds in range(1, sections):
        send(5, marg_out.at[ds], marg_in.at[sections - ds], at(0, 0, 0, ds))

    arrived(4, turned_in.at[pl.ds(1, sections - 1)])
    mine = functools.reduce(
        jnp.add, [turned_out[0].astype(jnp.float32)] + [turned_in[d].astype(jnp.float32) for d in range(1, sections)]
    )
    mine = (mine * (1.0 / sharp)).astype(jnp.bfloat16)
    with_one = jnp.concatenate([mine, jnp.ones((particles, LANES), jnp.bfloat16)], axis=1)
    arrived(5, marg_in.at[pl.ds(1, sections - 1)])
    parts = [marg_out[0]] + [marg_in[d] for d in range(1, sections)]
    largest = functools.reduce(jnp.maximum, parts)
    marg = largest + jnp.log(functools.reduce(jnp.add, [jnp.exp(one - largest) for one in parts]))
    highest = jnp.max(jnp.where(listed > 0.0, marg, -jnp.inf), axis=1, keepdims=True)
    weight = jnp.where(listed > 0.0, jnp.exp(marg - highest), 0.0)
    weight = (weight / jnp.sum(weight, axis=1, keepdims=True)).astype(jnp.bfloat16)
    sums = contract_first(weight, with_one)
    sum_x[...] = sums.astype(jnp.bfloat16).reshape(sum_x.shape)
    for dx in range(1, nx):
        send(6, sum_x.at[dx], got_x.at[dx], at(0, dx, 0, 0))

    peak = jnp.max(marg, axis=1, keepdims=True)
    proof = peak + jnp.log(jnp.sum(jnp.exp(marg - peak), axis=1, keepdims=True))
    evidence[...] = jnp.sum(jnp.where(eye, jnp.broadcast_to(proof, (particles, particles)), 0.0), axis=0, keepdims=True)

    arrived(6, got_x.at[pl.ds(1, nx - 1)])
    total = functools.reduce(
        jnp.add, [sum_x[0].astype(jnp.float32)] + [got_x[d].astype(jnp.float32) for d in range(1, nx)]
    )
    sum_y[...] = total.reshape(sum_y.shape).astype(jnp.bfloat16)
    for dy in range(1, ny):
        send(7, sum_y.at[dy], got_y.at[dy], at(0, 0, dy, 0))
    arrived(7, got_y.at[pl.ds(1, ny - 1)])
    total = functools.reduce(
        jnp.add, [sum_y[0].astype(jnp.float32)] + [got_y[d].astype(jnp.float32) for d in range(1, ny)]
    )
    for dz in range(nz):
        sum_z[dz] = total[2 * dz : 2 * dz + 2]
    for dz in range(nz):
        for ds in range(sections):
            if (dz, ds) != (0, 0):
                send(8, sum_z.at[dz], got_z.at[dz * sections + section], at(dz, 0, 0, ds))
    got_z[section] = sum_z[0]
    arrived(8, got_z.at[pl.ds(0, nz * sections - 1)])
    total = functools.reduce(jnp.add, [got_z[d] for d in range(nz * sections)])
    over = total[:, width:] + 1.0
    over = jnp.concatenate([over] * (width // LANES), axis=1)
    new_references[...] = (total[:, 0:width] + references[...].astype(jnp.float32)) / over

    sent(0, near.at[pl.ds(1, nz - 1)])
    sent(1, refs.at[0, pl.ds(1, ny - 1)])
    sent(2, refs.at[pl.ds(1, nx - 1)])
    sent(3, coef.at[pl.ds(1, sections - 1)])
    sent(4, turned_out.at[pl.ds(1, sections - 1)])
    sent(5, marg_out.at[pl.ds(1, sections - 1)])
    sent(6, sum_x.at[pl.ds(1, nx - 1)])
    sent(7, sum_y.at[pl.ds(1, ny - 1)])
    sent(8, got_z.at[pl.ds(0, nz * sections - 1)])


def body(
    dims,
    images,
    group_ids,
    row_filters,
    column_filters,
    basis_rows,
    basis_columns,
    rotations,
    references,
    sharpness,
    best_rotation,
    assignments,
):
    nz, nx, ny = dims
    sections = 4
    particles, pix = images.shape[0], images.shape[1]
    nb = basis_rows.shape[1]
    local, width = rotations.shape[0], rotations.shape[1]
    classes = 2 * nz * nx * ny
    wide = width + LANES
    bf16, f32 = jnp.bfloat16, jnp.float32
    hbm = pl.BlockSpec(memory_space=pltpu.HBM)
    vmem = pl.BlockSpec(memory_space=pltpu.VMEM)
    smem = pl.BlockSpec(memory_space=pltpu.SMEM)
    new_references, evidence = pl.pallas_call(
        functools.partial(kernel, dims),
        out_shape=(
            jax.ShapeDtypeStruct((2, width), f32),
            jax.ShapeDtypeStruct((1, particles), f32),
        ),
        in_specs=[hbm, smem, hbm, hbm, hbm, hbm, hbm, hbm, vmem, vmem, vmem, vmem],
        out_specs=(vmem, vmem),
        scratch_shapes=[
            pltpu.VMEM((particles, pix, pix), bf16),
            pltpu.VMEM(row_filters.shape, bf16),
            pltpu.VMEM(column_filters.shape, bf16),
            pltpu.VMEM((pix, pix), f32),
            pltpu.VMEM(rotations.shape, bf16),
            pltpu.VMEM((2, nb, pix), bf16),
            pltpu.VMEM((pix, nb * nb), bf16),
            pltpu.VMEM((pix, nb * nb), f32),
            pltpu.VMEM((particles, nb * nb), f32),
            pltpu.VMEM((particles, pix), f32),
            pltpu.VMEM((nz, 2, width), bf16),
            pltpu.VMEM((nx, ny, 2 * nz, width), bf16),
            pltpu.VMEM((sections, particles, wide), bf16),
            pltpu.VMEM((sections, particles, width), bf16),
            pltpu.VMEM((sections, particles, width), bf16),
            pltpu.VMEM((sections, particles, classes), f32),
            pltpu.VMEM((sections, particles, classes), f32),
            pltpu.VMEM((nx, 2 * ny * nz, wide), bf16),
            pltpu.VMEM((nx, 2 * ny * nz, wide), bf16),
            pltpu.VMEM((ny, 2 * nz, wide), bf16),
            pltpu.VMEM((ny, 2 * nz, wide), bf16),
            pltpu.VMEM((nz, 2, wide), f32),
            pltpu.VMEM((nz * sections, 2, wide), f32),
            pltpu.SemaphoreType.DMA((particles,)),
            pltpu.SemaphoreType.DMA((6,)),
            pltpu.SemaphoreType.DMA((9,)),
            pltpu.SemaphoreType.DMA((9,)),
        ],
        compiler_params=pltpu.CompilerParams(
            collective_id=0, has_side_effects=True, vmem_limit_bytes=63 * 1024 * 1024
        ),
    )(
        images,
        group_ids,
        row_filters,
        column_filters,
        basis_rows.T,
        basis_columns.T,
        jnp.asarray(soft_edge(pix)),
        rotations,
        references,
        sharpness.reshape(1, particles),
        best_rotation.reshape(1, particles),
        assignments,
    )
    return new_references, evidence.reshape(particles)


def solution(mesh, dims=TORUS):
    in_specs = (
        P(("section", "cls"), None, None),
        P(("section", "cls")),
        P(),
        P(),
        P(),
        P(),
        P("section", None, None),
        P("cls", None),
        P(("section", "cls")),
        P(("section", "cls")),
        P(("section", "cls"), None),
    )
    out_specs = (P("cls", None), P(("section", "cls")))
    return jax.shard_map(
        functools.partial(body, dims), mesh=mesh, in_specs=in_specs, out_specs=out_specs, check_vma=False
    )
```

```python
import functools
import math

import jax
import jax.numpy as jnp
import numpy as np
from jax import lax
from jax.experimental import pallas as pl
from jax.experimental.pallas import tpu as pltpu
from jax.sharding import PartitionSpec as P

EPSILON = 1e-05
TORUS = (4, 4, 8)
MESH = pl.DeviceIdType.MESH
LANES = 128


def soft_edge(pixels):
    coordinate = (np.arange(pixels, dtype=np.float32) - np.float32((pixels - 1) / 2.0)) / np.float32(pixels / 2.0)
    radius = np.sqrt(coordinate[:, None] * coordinate[:, None] + coordinate[None, :] * coordinate[None, :])
    falloff = np.clip((radius - np.float32(0.8)) / np.float32(0.15), 0.0, 1.0)
    return (0.5 + 0.5 * np.cos(math.pi * falloff)).astype(np.float32)


def contract_last(a, b):
    return lax.dot_general(a, b, (((1,), (1,)), ((), ())), preferred_element_type=jnp.float32)


def contract_first(a, b):
    return lax.dot_general(a, b, (((0,), (0,)), ((), ())), preferred_element_type=jnp.float32)


def kernel(
    dims,
    images,
    group_ids_hbm,
    row_filters,
    column_filters,
    basis_rows,
    basis_columns,
    mask,
    rotations,
    references_hbm,
    sharpness_hbm,
    best_rotation_hbm,
    assignments_hbm,
    new_references,
    evidence,
    img,
    rowf,
    colf,
    edge,
    rot,
    bas,
    tiled,
    spread,
    group_ids,
    references,
    sharpness,
    best_rotation,
    assignments,
    raw,
    squares,
    near,
    refs,
    coef,
    turned,
    turned_out,
    turned_in,
    marg_out,
    marg_in,
    sum_x,
    got_x,
    sum_y,
    got_y,
    sum_z,
    got_z,
    img_sem,
    in_sem,
    send_sem,
    recv_sem,
):
    nz, nx, ny = dims
    section, cls = lax.axis_index("section"), lax.axis_index("cls")
    sections = 4
    zh = cls // (nx * ny)
    xx = (cls // ny) % nx
    yy = cls % ny
    particles, pix = img.shape[0], img.shape[1]
    local = rot.shape[0]
    width = rot.shape[1]
    classes = nz * nx * ny * 2
    nb = bas.shape[1]

    def at(dz, dx, dy, ds):
        return {
            "section": (section + ds) % sections,
            "cls": (((zh + dz) % nz) * nx + (xx + dx) % nx) * ny + (yy + dy) % ny,
        }

    peers = [at(0, dx, 0, 0) for dx in range(1, nx)]
    peers += [at(0, 0, dy, 0) for dy in range(1, ny)]
    peers += [at(dz, 0, 0, ds) for dz in range(nz) for ds in range(sections) if (dz, ds) != (0, 0)]
    barrier = pltpu.get_barrier_semaphore()
    for peer in peers:
        pl.semaphore_signal(barrier, inc=1, device_id=peer, device_id_type=MESH)

    inputs = {}
    for k, (src, dst) in enumerate(
        [
            (column_filters, colf),
            (row_filters, rowf),
            (basis_rows, bas.at[0]),
            (basis_columns, bas.at[1]),
            (mask, edge),
            (rotations, rot),
            (group_ids_hbm, group_ids),
            (references_hbm, references),
            (sharpness_hbm, sharpness),
            (best_rotation_hbm, best_rotation),
            (assignments_hbm, assignments),
        ]
    ):
        inputs[k] = pltpu.make_async_copy(src, dst, in_sem.at[k])
    for k in (2, 3, 6, 0):
        inputs[k].start()
    pltpu.make_async_copy(images.at[0], img.at[0], img_sem.at[0]).start()
    for k in (1, 4, 7):
        inputs[k].start()

    @pl.loop(1, particles)
    def _(n):
        pltpu.make_async_copy(images.at[n], img.at[n], img_sem.at[n]).start()

    for k in (8, 9, 10):
        inputs[k].start()
    inputs[5].start()

    inputs[2].wait()
    inputs[3].wait()
    row_at = lax.broadcasted_iota(jnp.int32, (nb, nb * nb), 0)
    lane_at = lax.broadcasted_iota(jnp.int32, (nb, nb * nb), 1)
    minor = (lane_at % nb == row_at).astype(jnp.float32).astype(jnp.bfloat16)
    major = (lane_at // nb == row_at).astype(jnp.float32).astype(jnp.bfloat16)
    tiled[...] = contract_first(bas[1], minor).astype(jnp.bfloat16)
    spread[...] = contract_first(bas[0], major)
    inputs[0].wait()
    inputs[1].wait()
    inputs[4].wait()
    inputs[6].wait()

    def filter_images(low, high, together):
        @pl.loop(low, high, step=together)
        def _(n):
            some = [n + k for k in range(together)]
            halves = []
            for m in some:
                pltpu.make_async_copy(images.at[m], img.at[m], img_sem.at[m]).wait()
                half = jnp.dot(img[m], colf[group_ids[m]], preferred_element_type=jnp.float32)
                halves.append(half.astype(jnp.bfloat16))
            masked = [
                jnp.dot(rowf[group_ids[m]], half, preferred_element_type=jnp.float32) * edge[...]
                for m, half in zip(some, halves)
            ]
            for m, one in zip(some, masked):
                squares[pl.ds(m, 1), :] = jnp.sum(one * one, axis=0, keepdims=True)
            inner = [jnp.dot(one.astype(jnp.bfloat16), tiled[...], preferred_element_type=jnp.float32) for one in masked]
            for m, one in zip(some, inner):
                raw[pl.ds(m, 1), :] = jnp.sum(one * spread[...], axis=0, keepdims=True)

    def send(k, src, dst, to):
        pltpu.make_async_remote_copy(
            src_ref=src,
            dst_ref=dst,
            send_sem=send_sem.at[k],
            recv_sem=recv_sem.at[k],
            device_id=to,
            device_id_type=MESH,
        ).start()

    def arrived(k, ref):
        pltpu.make_async_copy(ref, ref, recv_sem.at[k]).wait()

    def sent(k, ref):
        pltpu.make_async_copy(ref, ref, send_sem.at[k]).wait()

    filter_images(0, particles // 2, 4)

    pl.semaphore_wait(barrier, len(peers))
    inputs[7].wait()
    near[0] = references[...]
    zl, core = section // 2, section % 2
    toward = 2 * zl - 1 + nz
    for dz, low, slot in ((toward, zl, 1 + (nz - 2) * zl), (toward, 1 - zl, 1 + (nz - 2) * zl), (2, 1 - zl, 2)):
        to = {"section": low * 2 + core, "cls": (((zh + dz) % nz) * nx + xx) * ny + yy}
        send(0, near.at[0], near.at[slot], to)
    filter_images(particles // 2, particles, 4)

    eye = lax.broadcasted_iota(jnp.int32, (particles, particles), 0) == lax.broadcasted_iota(
        jnp.int32, (particles, particles), 1
    )
    inputs[8].wait()
    inputs[9].wait()
    sharp_row = sharpness[...].astype(jnp.float32)
    sharp = jnp.sum(jnp.where(eye, jnp.broadcast_to(sharp_row, (particles, particles)), 0.0), axis=1, keepdims=True)
    best_row = best_rotation[...].astype(jnp.float32)
    best = jnp.sum(jnp.where(eye, jnp.broadcast_to(best_row, (particles, particles)), 0.0), axis=1, keepdims=True)
    power = jnp.sum(squares[...], axis=1, keepdims=True) * (1.0 / (pix * pix))
    scale = lax.rsqrt(power + EPSILON) * sharp
    coef[0, :, 0:width] = (raw[...] * scale).astype(jnp.bfloat16)
    coef[0, :, width:] = jnp.broadcast_to(best, (particles, LANES)).astype(jnp.bfloat16)
    for ds in range(1, sections):
        send(3, coef.at[0], coef.at[sections - ds], at(0, 0, 0, ds))

    arrived(0, near.at[pl.ds(1, nz - 1)])
    refs[0, 0] = jnp.concatenate([near[dz].astype(jnp.float32) for dz in range(nz)], axis=0).astype(jnp.bfloat16)
    for dy in range(1, ny):
        send(1, refs.at[0, 0], refs.at[0, ny - dy], at(0, 0, dy, 0))

    place = lax.broadcasted_iota(jnp.int32, (particles, classes), 1)
    dx_at, rest = place // (ny * nz * 2), place % (ny * nz * 2)
    dy_at, rest = rest // (nz * 2), rest % (nz * 2)
    dz_at, last = rest // 2, rest % 2
    name = ((((zh + dz_at) % nz) * nx + (xx + dx_at) % nx) * ny + (yy + dy_at) % ny) * 2 + last
    inputs[10].wait()
    listed = jnp.zeros((particles, classes), jnp.float32)
    for j in range(assignments.shape[1]):
        listed = jnp.where(assignments[:, j : j + 1] == name, 1.0, listed)

    inputs[5].wait()
    arrived(3, coef.at[pl.ds(1, sections - 1)])
    everyone = sections * particles
    gathered = coef[:, :, 0:width].reshape(everyone, width)
    best_all = coef[:, :, width:].astype(jnp.float32).reshape(everyone, LANES)
    best_all = jnp.concatenate([best_all] * (width // LANES), axis=1)
    first = (section * local).astype(jnp.float32)
    aligned = jnp.zeros((everyone, width), jnp.float32)
    for r in range(local):
        one = contract_last(gathered, rot[r])
        aligned = jnp.where(best_all == first + float(r), one, aligned)
        turned[pl.ds(r * everyone, everyone), :] = one.astype(jnp.bfloat16)
    turned_out[...] = aligned.astype(jnp.bfloat16).reshape(sections, particles, width)
    for ds in range(1, sections):
        send(4, turned_out.at[ds], turned_in.at[sections - ds], at(0, 0, 0, ds))

    arrived(1, refs.at[0, pl.ds(1, ny - 1)])
    for dx in range(1, nx):
        send(2, refs.at[0], refs.at[nx - dx], at(0, dx, 0, 0))
    arrived(4, turned_in.at[pl.ds(1, sections - 1)])
    mine = functools.reduce(
        jnp.add, [turned_out[0].astype(jnp.float32)] + [turned_in[d].astype(jnp.float32) for d in range(1, sections)]
    )
    mine = (mine * (1.0 / sharp)).astype(jnp.bfloat16)
    with_one = jnp.concatenate([mine, jnp.ones((particles, LANES), jnp.bfloat16)], axis=1)

    arrived(2, refs.at[pl.ds(1, nx - 1)])
    all_refs = refs[...].astype(jnp.float32).reshape(classes, width).astype(jnp.bfloat16)
    scores = contract_last(turned[...], all_refs).reshape(local, everyone, classes)
    largest = jnp.max(scores, axis=0)
    total = jnp.sum(jnp.exp(scores - largest), axis=0)
    marg_out[...] = (largest + jnp.log(total)).reshape(sections, particles, classes)
    for ds in range(1, sections):
        send(5, marg_out.at[ds], marg_in.at[sections - ds], at(0, 0, 0, ds))
    arrived(5, marg_in.at[pl.ds(1, sections - 1)])
    parts = [marg_out[0]] + [marg_in[d] for d in range(1, sections)]
    largest = functools.reduce(jnp.maximum, parts)
    marg = largest + jnp.log(functools.reduce(jnp.add, [jnp.exp(one - largest) for one in parts]))
    highest = jnp.max(jnp.where(listed > 0.0, marg, -jnp.inf), axis=1, keepdims=True)
    weight = jnp.where(listed > 0.0, jnp.exp(marg - highest), 0.0)
    weight = (weight / jnp.sum(weight, axis=1, keepdims=True)).astype(jnp.bfloat16)
    sums = contract_first(weight, with_one)
    sum_x[...] = sums.astype(jnp.bfloat16).reshape(sum_x.shape)
    for dx in range(1, nx):
        send(6, sum_x.at[dx], got_x.at[dx], at(0, dx, 0, 0))

    peak = jnp.max(marg, axis=1, keepdims=True)
    proof = peak + jnp.log(jnp.sum(jnp.exp(marg - peak), axis=1, keepdims=True))
    evidence[...] = jnp.sum(jnp.where(eye, jnp.broadcast_to(proof, (particles, particles)), 0.0), axis=0, keepdims=True)

    arrived(6, got_x.at[pl.ds(1, nx - 1)])
    total = functools.reduce(
        jnp.add, [sum_x[0].astype(jnp.float32)] + [got_x[d].astype(jnp.float32) for d in range(1, nx)]
    )
    sum_y[...] = total.reshape(sum_y.shape).astype(jnp.bfloat16)
    for dy in range(1, ny):
        send(7, sum_y.at[dy], got_y.at[dy], at(0, 0, dy, 0))
    arrived(7, got_y.at[pl.ds(1, ny - 1)])
    total = functools.reduce(
        jnp.add, [sum_y[0].astype(jnp.float32)] + [got_y[d].astype(jnp.float32) for d in range(1, ny)]
    )
    for dz in range(nz):
        sum_z[dz] = total[2 * dz : 2 * dz + 2]
    for dz in range(nz):
        for ds in range(sections):
            if (dz, ds) != (0, 0):
                send(8, sum_z.at[dz], got_z.at[dz * sections + section], at(dz, 0, 0, ds))
    got_z[section] = sum_z[0]
    arrived(8, got_z.at[pl.ds(0, nz * sections - 1)])
    total = functools.reduce(jnp.add, [got_z[d] for d in range(nz * sections)])
    over = total[:, width:] + 1.0
    over = jnp.concatenate([over] * (width // LANES), axis=1)
    new_references[...] = (total[:, 0:width] + references[...].astype(jnp.float32)) / over

    sent(0, near.at[pl.ds(1, nz - 1)])
    sent(1, refs.at[0, pl.ds(1, ny - 1)])
    sent(2, refs.at[pl.ds(1, nx - 1)])
    sent(3, coef.at[pl.ds(1, sections - 1)])
    sent(4, turned_out.at[pl.ds(1, sections - 1)])
    sent(5, marg_out.at[pl.ds(1, sections - 1)])
    sent(6, sum_x.at[pl.ds(1, nx - 1)])
    sent(7, sum_y.at[pl.ds(1, ny - 1)])
    sent(8, got_z.at[pl.ds(0, nz * sections - 1)])


def hand_on(sums, proofs, new_references, evidence, sems):
    copies = [
        pltpu.make_async_copy(sums, new_references, sems.at[0]),
        pltpu.make_async_copy(proofs, evidence, sems.at[1]),
    ]
    for copy in copies:
        copy.start()
    for copy in copies:
        copy.wait()


def body(
    dims,
    images,
    group_ids,
    row_filters,
    column_filters,
    basis_rows,
    basis_columns,
    rotations,
    references,
    sharpness,
    best_rotation,
    assignments,
):
    nz, nx, ny = dims
    sections = 4
    particles, pix = images.shape[0], images.shape[1]
    nb = basis_rows.shape[1]
    local, width = rotations.shape[0], rotations.shape[1]
    classes = 2 * nz * nx * ny
    wide = width + LANES
    bf16, f32 = jnp.bfloat16, jnp.float32
    hbm = pl.BlockSpec(memory_space=pltpu.HBM)
    vmem = pl.BlockSpec(memory_space=pltpu.VMEM)
    new_references, evidence = pl.pallas_call(
        functools.partial(kernel, dims),
        out_shape=(
            jax.ShapeDtypeStruct((2, width), f32),
            jax.ShapeDtypeStruct((1, particles), f32),
        ),
        in_specs=[hbm] * 12,
        out_specs=(vmem, vmem),
        scratch_shapes=[
            pltpu.VMEM((particles, pix, pix), bf16),
            pltpu.VMEM(row_filters.shape, bf16),
            pltpu.VMEM(column_filters.shape, bf16),
            pltpu.VMEM((pix, pix), f32),
            pltpu.VMEM(rotations.shape, bf16),
            pltpu.VMEM((2, nb, pix), bf16),
            pltpu.VMEM((pix, nb * nb), bf16),
            pltpu.VMEM((pix, nb * nb), f32),
            pltpu.SMEM((particles,), jnp.int32),
            pltpu.VMEM((2, width), bf16),
            pltpu.VMEM((1, particles), bf16),
            pltpu.VMEM((1, particles), jnp.int32),
            pltpu.VMEM(assignments.shape, jnp.int32),
            pltpu.VMEM((particles, nb * nb), f32),
            pltpu.VMEM((particles, pix), f32),
            pltpu.VMEM((nz, 2, width), bf16),
            pltpu.VMEM((nx, ny, 2 * nz, width), bf16),
            pltpu.VMEM((sections, particles, wide), bf16),
            pltpu.VMEM((local * sections * particles, width), bf16),
            pltpu.VMEM((sections, particles, width), bf16),
            pltpu.VMEM((sections, particles, width), bf16),
            pltpu.VMEM((sections, particles, classes), f32),
            pltpu.VMEM((sections, particles, classes), f32),
            pltpu.VMEM((nx, 2 * ny * nz, wide), bf16),
            pltpu.VMEM((nx, 2 * ny * nz, wide), bf16),
            pltpu.VMEM((ny, 2 * nz, wide), bf16),
            pltpu.VMEM((ny, 2 * nz, wide), bf16),
            pltpu.VMEM((nz, 2, wide), f32),
            pltpu.VMEM((nz * sections, 2, wide), f32),
            pltpu.SemaphoreType.DMA((particles,)),
            pltpu.SemaphoreType.DMA((11,)),
            pltpu.SemaphoreType.DMA((9,)),
            pltpu.SemaphoreType.DMA((9,)),
        ],
        compiler_params=pltpu.CompilerParams(
            collective_id=0, has_side_effects=True, vmem_limit_bytes=63 * 1024 * 1024
        ),
    )(
        images,
        group_ids,
        row_filters,
        column_filters,
        basis_rows.T,
        basis_columns.T,
        jnp.asarray(soft_edge(pix)),
        rotations,
        references,
        sharpness.reshape(1, particles),
        best_rotation.reshape(1, particles),
        assignments,
    )
    new_references, evidence = pl.pallas_call(
        hand_on,
        out_shape=(
            jax.ShapeDtypeStruct((2, width), f32),
            jax.ShapeDtypeStruct((1, particles), f32),
        ),
        in_specs=[hbm, hbm],
        out_specs=(hbm, hbm),
        scratch_shapes=[pltpu.SemaphoreType.DMA((2,))],
    )(new_references, evidence)
    return new_references, evidence.reshape(particles)


def solution(mesh, dims=TORUS):
    in_specs = (
        P(("section", "cls"), None, None),
        P(("section", "cls")),
        P(),
        P(),
        P(),
        P(),
        P("section", None, None),
        P("cls", None),
        P(("section", "cls")),
        P(("section", "cls")),
        P(("section", "cls"), None),
    )
    out_specs = (P("cls", None), P(("section", "cls")))
    return jax.shard_map(
        functools.partial(body, dims), mesh=mesh, in_specs=in_specs, out_specs=out_specs, check_vma=False
    )
```

```python
import functools
import math

import jax
import jax.numpy as jnp
import numpy as np
from jax import lax
from jax.experimental import pallas as pl
from jax.experimental.pallas import tpu as pltpu
from jax.sharding import PartitionSpec as P

EPSILON = 1e-05
TORUS = (4, 4, 8)
MESH = pl.DeviceIdType.MESH
LANES = 128


def soft_edge(pixels):
    coordinate = (np.arange(pixels, dtype=np.float32) - np.float32((pixels - 1) / 2.0)) / np.float32(pixels / 2.0)
    radius = np.sqrt(coordinate[:, None] * coordinate[:, None] + coordinate[None, :] * coordinate[None, :])
    falloff = np.clip((radius - np.float32(0.8)) / np.float32(0.15), 0.0, 1.0)
    return (0.5 + 0.5 * np.cos(math.pi * falloff)).astype(np.float32)


def contract_last(a, b):
    return lax.dot_general(a, b, (((1,), (1,)), ((), ())), preferred_element_type=jnp.float32)


def contract_first(a, b):
    return lax.dot_general(a, b, (((0,), (0,)), ((), ())), preferred_element_type=jnp.float32)


def kernel(
    dims,
    images,
    group_ids_hbm,
    row_filters,
    column_filters,
    basis_rows,
    basis_columns,
    mask,
    rotations,
    references_hbm,
    sharpness_hbm,
    best_rotation_hbm,
    assignments_hbm,
    new_references,
    evidence,
    img,
    rowf,
    colf,
    edge,
    rot,
    bas,
    tiled,
    spread,
    group_ids,
    references,
    sharpness,
    best_rotation,
    assignments,
    raw,
    squares,
    near,
    refs,
    coef,
    turned,
    turned_out,
    turned_in,
    marg_out,
    marg_in,
    sum_y,
    got_y,
    sum_z,
    got_z,
    img_sem,
    in_sem,
    send_sem,
    recv_sem,
):
    nz, nx, ny = dims
    section, cls = lax.axis_index("section"), lax.axis_index("cls")
    sections = 4
    zh = cls // (nx * ny)
    xx = (cls // ny) % nx
    yy = cls % ny
    particles, pix = img.shape[0], img.shape[1]
    local = rot.shape[0]
    width = rot.shape[1]
    classes = nz * nx * ny * 2
    nb = bas.shape[1]

    def at(dz, dx, dy, ds):
        return {
            "section": (section + ds) % sections,
            "cls": (((zh + dz) % nz) * nx + (xx + dx) % nx) * ny + (yy + dy) % ny,
        }

    peers = [at(0, dx, 0, 0) for dx in range(1, nx)]
    peers += [at(0, 0, dy, 0) for dy in range(1, ny)]
    peers += [at(dz, 0, 0, ds) for dz in range(nz) for ds in range(sections) if (dz, ds) != (0, 0)]
    barrier = pltpu.get_barrier_semaphore()
    for peer in peers:
        pl.semaphore_signal(barrier, inc=1, device_id=peer, device_id_type=MESH)

    inputs = {}
    for k, (src, dst) in enumerate(
        [
            (column_filters, colf),
            (row_filters, rowf),
            (basis_rows, bas.at[0]),
            (basis_columns, bas.at[1]),
            (mask, edge),
            (rotations, rot),
            (group_ids_hbm, group_ids),
            (references_hbm, references),
            (sharpness_hbm, sharpness),
            (best_rotation_hbm, best_rotation),
            (assignments_hbm, assignments),
        ]
    ):
        inputs[k] = pltpu.make_async_copy(src, dst, in_sem.at[k])
    for k in (2, 3, 6, 0):
        inputs[k].start()
    pltpu.make_async_copy(images.at[0], img.at[0], img_sem.at[0]).start()
    for k in (1, 4, 7):
        inputs[k].start()

    @pl.loop(1, particles)
    def _(n):
        pltpu.make_async_copy(images.at[n], img.at[n], img_sem.at[n]).start()

    for k in (8, 9, 10):
        inputs[k].start()
    inputs[5].start()

    inputs[2].wait()
    inputs[3].wait()
    row_at = lax.broadcasted_iota(jnp.int32, (nb, nb * nb), 0)
    lane_at = lax.broadcasted_iota(jnp.int32, (nb, nb * nb), 1)
    minor = (lane_at % nb == row_at).astype(jnp.float32).astype(jnp.bfloat16)
    major = (lane_at // nb == row_at).astype(jnp.float32).astype(jnp.bfloat16)
    tiled[...] = contract_first(bas[1], minor).astype(jnp.bfloat16)
    spread[...] = contract_first(bas[0], major)
    inputs[0].wait()
    inputs[1].wait()
    inputs[4].wait()
    inputs[6].wait()

    def filter_images(low, high, together):
        @pl.loop(low, high, step=together)
        def _(n):
            some = [n + k for k in range(together)]
            halves = []
            for m in some:
                pltpu.make_async_copy(images.at[m], img.at[m], img_sem.at[m]).wait()
                half = jnp.dot(img[m], colf[group_ids[m]], preferred_element_type=jnp.float32)
                halves.append(half.astype(jnp.bfloat16))
            masked = [
                jnp.dot(rowf[group_ids[m]], half, preferred_element_type=jnp.float32) * edge[...]
                for m, half in zip(some, halves)
            ]
            for m, one in zip(some, masked):
                squares[pl.ds(m, 1), :] = jnp.sum(one * one, axis=0, keepdims=True)
            inner = [jnp.dot(one.astype(jnp.bfloat16), tiled[...], preferred_element_type=jnp.float32) for one in masked]
            for m, one in zip(some, inner):
                raw[pl.ds(m, 1), :] = jnp.sum(one * spread[...], axis=0, keepdims=True)

    def send(k, src, dst, to):
        pltpu.make_async_remote_copy(
            src_ref=src,
            dst_ref=dst,
            send_sem=send_sem.at[k],
            recv_sem=recv_sem.at[k],
            device_id=to,
            device_id_type=MESH,
        ).start()

    def arrived(k, ref):
        pltpu.make_async_copy(ref, ref, recv_sem.at[k]).wait()

    def sent(k, ref):
        pltpu.make_async_copy(ref, ref, send_sem.at[k]).wait()

    filter_images(0, particles // 2, 4)

    pl.semaphore_wait(barrier, len(peers))
    inputs[7].wait()
    near[0] = references[...]
    zl, core = section // 2, section % 2
    toward = 2 * zl - 1 + nz
    for dz, low, slot in ((toward, zl, 1 + (nz - 2) * zl), (toward, 1 - zl, 1 + (nz - 2) * zl), (2, 1 - zl, 2)):
        to = {"section": low * 2 + core, "cls": (((zh + dz) % nz) * nx + xx) * ny + yy}
        send(0, near.at[0], near.at[slot], to)
    filter_images(particles // 2, particles, 4)

    eye = lax.broadcasted_iota(jnp.int32, (particles, particles), 0) == lax.broadcasted_iota(
        jnp.int32, (particles, particles), 1
    )
    inputs[8].wait()
    inputs[9].wait()
    sharp_row = sharpness[...].astype(jnp.float32)
    sharp = jnp.sum(jnp.where(eye, jnp.broadcast_to(sharp_row, (particles, particles)), 0.0), axis=1, keepdims=True)
    best_row = best_rotation[...].astype(jnp.float32)
    best = jnp.sum(jnp.where(eye, jnp.broadcast_to(best_row, (particles, particles)), 0.0), axis=1, keepdims=True)
    power = jnp.sum(squares[...], axis=1, keepdims=True) * (1.0 / (pix * pix))
    scale = lax.rsqrt(power + EPSILON) * sharp
    coef[0, :, 0:width] = (raw[...] * scale).astype(jnp.bfloat16)
    coef[0, :, width:] = jnp.broadcast_to(best, (particles, LANES)).astype(jnp.bfloat16)
    for ds in range(1, sections):
        send(3, coef.at[0], coef.at[sections - ds], at(0, 0, 0, ds))

    arrived(0, near.at[pl.ds(1, nz - 1)])
    refs[0, 0] = jnp.concatenate([near[dz].astype(jnp.float32) for dz in range(nz)], axis=0).astype(jnp.bfloat16)
    for dy in range(1, ny):
        send(1, refs.at[0, 0], refs.at[0, ny - dy], at(0, 0, dy, 0))

    place = lax.broadcasted_iota(jnp.int32, (particles, classes), 1)
    dx_at, rest = place // (ny * nz * 2), place % (ny * nz * 2)
    dy_at, rest = rest // (nz * 2), rest % (nz * 2)
    dz_at, last = rest // 2, rest % 2
    name = ((((zh + dz_at) % nz) * nx + (xx + dx_at) % nx) * ny + (yy + dy_at) % ny) * 2 + last
    inputs[10].wait()
    listed = jnp.zeros((particles, classes), jnp.float32)
    for j in range(assignments.shape[1]):
        listed = jnp.where(assignments[:, j : j + 1] == name, 1.0, listed)

    inputs[5].wait()
    arrived(3, coef.at[pl.ds(1, sections - 1)])
    everyone = sections * particles
    gathered = coef[:, :, 0:width].reshape(everyone, width)
    best_all = coef[:, :, width:].astype(jnp.float32).reshape(everyone, LANES)
    best_all = jnp.concatenate([best_all] * (width // LANES), axis=1)
    first = (section * local).astype(jnp.float32)
    aligned = jnp.zeros((everyone, width), jnp.float32)
    for r in range(local):
        one = contract_last(gathered, rot[r])
        aligned = jnp.where(best_all == first + float(r), one, aligned)
        turned[pl.ds(r * everyone, everyone), :] = one.astype(jnp.bfloat16)
    turned_out[...] = aligned.astype(jnp.bfloat16).reshape(sections, particles, width)
    for ds in range(1, sections):
        send(4, turned_out.at[ds], turned_in.at[sections - ds], at(0, 0, 0, ds))

    arrived(1, refs.at[0, pl.ds(1, ny - 1)])
    for dx in range(1, nx):
        send(2, refs.at[0], refs.at[nx - dx], at(0, dx, 0, 0))
    arrived(4, turned_in.at[pl.ds(1, sections - 1)])
    mine = functools.reduce(
        jnp.add, [turned_out[0].astype(jnp.float32)] + [turned_in[d].astype(jnp.float32) for d in range(1, sections)]
    )
    mine = (mine * (1.0 / sharp)).astype(jnp.bfloat16)
    with_one = jnp.concatenate([mine, jnp.ones((particles, LANES), jnp.bfloat16)], axis=1)

    arrived(2, refs.at[pl.ds(1, nx - 1)])
    all_refs = refs[...].astype(jnp.float32).reshape(classes, width).astype(jnp.bfloat16)
    scores = contract_last(turned[...], all_refs).reshape(local, everyone, classes)
    largest = jnp.max(scores, axis=0)
    total = jnp.sum(jnp.exp(scores - largest), axis=0)
    marg_out[...] = (largest + jnp.log(total)).reshape(sections, particles, classes)
    for ds in range(1, sections):
        send(5, marg_out.at[ds], marg_in.at[sections - ds], at(0, 0, 0, ds))
    arrived(5, marg_in.at[pl.ds(1, sections - 1)])
    parts = [marg_out[0]] + [marg_in[d] for d in range(1, sections)]
    largest = functools.reduce(jnp.maximum, parts)
    marg = largest + jnp.log(functools.reduce(jnp.add, [jnp.exp(one - largest) for one in parts]))
    highest = jnp.max(jnp.where(listed > 0.0, marg, -jnp.inf), axis=1, keepdims=True)
    weight = jnp.where(listed > 0.0, jnp.exp(marg - highest), 0.0)
    weight = (weight / jnp.sum(weight, axis=1, keepdims=True)).astype(jnp.bfloat16)
    sums = contract_first(weight, with_one)
    sum_y[...] = sums.reshape(sum_y.shape).astype(jnp.bfloat16)
    order = [(dx, dy) for dx in range(nx) for dy in range(ny) if (dx, dy) != (0, 0)]
    for dx, dy in sorted(order, key=lambda d: -min(d[0], nx - d[0]) - min(d[1], ny - d[1])):
        send(6, sum_y.at[dx * ny + dy], got_y.at[dx * ny + dy], at(0, dx, dy, 0))

    peak = jnp.max(marg, axis=1, keepdims=True)
    proof = peak + jnp.log(jnp.sum(jnp.exp(marg - peak), axis=1, keepdims=True))
    evidence[...] = jnp.sum(jnp.where(eye, jnp.broadcast_to(proof, (particles, particles)), 0.0), axis=0, keepdims=True)

    arrived(6, got_y.at[pl.ds(1, nx * ny - 1)])
    total = functools.reduce(
        jnp.add, [sum_y[0].astype(jnp.float32)] + [got_y[d].astype(jnp.float32) for d in range(1, nx * ny)]
    )
    for dz in range(nz):
        sum_z[dz] = total[2 * dz : 2 * dz + 2]
    for dz in range(nz):
        for ds in range(sections):
            if (dz, ds) != (0, 0):
                send(7, sum_z.at[dz], got_z.at[dz * sections + section], at(dz, 0, 0, ds))
    got_z[section] = sum_z[0]
    arrived(7, got_z.at[pl.ds(0, nz * sections - 1)])
    total = functools.reduce(jnp.add, [got_z[d] for d in range(nz * sections)])
    over = total[:, width:] + 1.0
    over = jnp.concatenate([over] * (width // LANES), axis=1)
    new_references[...] = (total[:, 0:width] + references[...].astype(jnp.float32)) / over

    sent(0, near.at[pl.ds(1, nz - 1)])
    sent(1, refs.at[0, pl.ds(1, ny - 1)])
    sent(2, refs.at[pl.ds(1, nx - 1)])
    sent(3, coef.at[pl.ds(1, sections - 1)])
    sent(4, turned_out.at[pl.ds(1, sections - 1)])
    sent(5, marg_out.at[pl.ds(1, sections - 1)])
    sent(6, sum_y.at[pl.ds(1, nx * ny - 1)])
    sent(7, got_z.at[pl.ds(0, nz * sections - 1)])


def hand_on(sums, proofs, new_references, evidence, sems):
    copies = [
        pltpu.make_async_copy(sums, new_references, sems.at[0]),
        pltpu.make_async_copy(proofs, evidence, sems.at[1]),
    ]
    for copy in copies:
        copy.start()
    for copy in copies:
        copy.wait()


def body(
    dims,
    images,
    group_ids,
    row_filters,
    column_filters,
    basis_rows,
    basis_columns,
    rotations,
    references,
    sharpness,
    best_rotation,
    assignments,
):
    nz, nx, ny = dims
    sections = 4
    particles, pix = images.shape[0], images.shape[1]
    nb = basis_rows.shape[1]
    local, width = rotations.shape[0], rotations.shape[1]
    classes = 2 * nz * nx * ny
    wide = width + LANES
    bf16, f32 = jnp.bfloat16, jnp.float32
    hbm = pl.BlockSpec(memory_space=pltpu.HBM)
    vmem = pl.BlockSpec(memory_space=pltpu.VMEM)
    new_references, evidence = pl.pallas_call(
        functools.partial(kernel, dims),
        out_shape=(
            jax.ShapeDtypeStruct((2, width), f32),
            jax.ShapeDtypeStruct((1, particles), f32),
        ),
        in_specs=[hbm] * 12,
        out_specs=(vmem, vmem),
        scratch_shapes=[
            pltpu.VMEM((particles, pix, pix), bf16),
            pltpu.VMEM(row_filters.shape, bf16),
            pltpu.VMEM(column_filters.shape, bf16),
            pltpu.VMEM((pix, pix), f32),
            pltpu.VMEM(rotations.shape, bf16),
            pltpu.VMEM((2, nb, pix), bf16),
            pltpu.VMEM((pix, nb * nb), bf16),
            pltpu.VMEM((pix, nb * nb), f32),
            pltpu.SMEM((particles,), jnp.int32),
            pltpu.VMEM((2, width), bf16),
            pltpu.VMEM((1, particles), bf16),
            pltpu.VMEM((1, particles), jnp.int32),
            pltpu.VMEM(assignments.shape, jnp.int32),
            pltpu.VMEM((particles, nb * nb), f32),
            pltpu.VMEM((particles, pix), f32),
            pltpu.VMEM((nz, 2, width), bf16),
            pltpu.VMEM((nx, ny, 2 * nz, width), bf16),
            pltpu.VMEM((sections, particles, wide), bf16),
            pltpu.VMEM((local * sections * particles, width), bf16),
            pltpu.VMEM((sections, particles, width), bf16),
            pltpu.VMEM((sections, particles, width), bf16),
            pltpu.VMEM((sections, particles, classes), f32),
            pltpu.VMEM((sections, particles, classes), f32),
            pltpu.VMEM((nx * ny, 2 * nz, wide), bf16),
            pltpu.VMEM((nx * ny, 2 * nz, wide), bf16),
            pltpu.VMEM((nz, 2, wide), f32),
            pltpu.VMEM((nz * sections, 2, wide), f32),
            pltpu.SemaphoreType.DMA((particles,)),
            pltpu.SemaphoreType.DMA((11,)),
            pltpu.SemaphoreType.DMA((8,)),
            pltpu.SemaphoreType.DMA((8,)),
        ],
        compiler_params=pltpu.CompilerParams(
            collective_id=0, has_side_effects=True, vmem_limit_bytes=63 * 1024 * 1024
        ),
    )(
        images,
        group_ids,
        row_filters,
        column_filters,
        basis_rows.T,
        basis_columns.T,
        jnp.asarray(soft_edge(pix)),
        rotations,
        references,
        sharpness.reshape(1, particles),
        best_rotation.reshape(1, particles),
        assignments,
    )
    new_references, evidence = pl.pallas_call(
        hand_on,
        out_shape=(
            jax.ShapeDtypeStruct((2, width), f32),
            jax.ShapeDtypeStruct((1, particles), f32),
        ),
        in_specs=[hbm, hbm],
        out_specs=(hbm, hbm),
        scratch_shapes=[pltpu.SemaphoreType.DMA((2,))],
    )(new_references, evidence)
    return new_references, evidence.reshape(particles)


def solution(mesh, dims=TORUS):
    in_specs = (
        P(("section", "cls"), None, None),
        P(("section", "cls")),
        P(),
        P(),
        P(),
        P(),
        P("section", None, None),
        P("cls", None),
        P(("section", "cls")),
        P(("section", "cls")),
        P(("section", "cls"), None),
    )
    out_specs = (P("cls", None), P(("section", "cls")))
    return jax.shard_map(
        functools.partial(body, dims), mesh=mesh, in_specs=in_specs, out_specs=out_specs, check_vma=False
    )
```

```python
import functools
import math

import jax
import jax.numpy as jnp
import numpy as np
from jax import lax
from jax.experimental import pallas as pl
from jax.experimental.pallas import tpu as pltpu
from jax.sharding import PartitionSpec as P

EPSILON = 1e-05
TORUS = (4, 4, 8)
MESH = pl.DeviceIdType.MESH
LANES = 128


def soft_edge(pixels):
    coordinate = (np.arange(pixels, dtype=np.float32) - np.float32((pixels - 1) / 2.0)) / np.float32(pixels / 2.0)
    radius = np.sqrt(coordinate[:, None] * coordinate[:, None] + coordinate[None, :] * coordinate[None, :])
    falloff = np.clip((radius - np.float32(0.8)) / np.float32(0.15), 0.0, 1.0)
    return (0.5 + 0.5 * np.cos(math.pi * falloff)).astype(np.float32)


def contract_last(a, b):
    return lax.dot_general(a, b, (((1,), (1,)), ((), ())), preferred_element_type=jnp.float32)


def contract_first(a, b):
    return lax.dot_general(a, b, (((0,), (0,)), ((), ())), preferred_element_type=jnp.float32)


def kernel(
    dims,
    images,
    group_ids_hbm,
    row_filters,
    column_filters,
    basis_rows,
    basis_columns,
    mask,
    rotations,
    references_hbm,
    sharpness_hbm,
    best_rotation_hbm,
    assignments_hbm,
    new_references,
    evidence,
    img,
    rowf,
    colf,
    edge,
    rot,
    bas,
    tiled,
    spread,
    group_ids,
    references,
    sharpness,
    best_rotation,
    assignments,
    raw,
    squares,
    near,
    refs,
    reorder,
    coef,
    turned,
    turned_out,
    turned_in,
    marg_out,
    marg_in,
    sum_y,
    got_y,
    sum_z,
    got_z,
    img_sem,
    in_sem,
    send_sem,
    recv_sem,
    ready,
):
    nz, nx, ny = dims
    section, cls = lax.axis_index("section"), lax.axis_index("cls")
    sections = 4
    zh = cls // (nx * ny)
    xx = (cls // ny) % nx
    yy = cls % ny
    particles, pix = img.shape[0], img.shape[1]
    local = rot.shape[0]
    width = rot.shape[1]
    classes = nz * nx * ny * 2
    nb = bas.shape[1]

    def at(dz, dx, dy, ds):
        return {
            "section": (section + ds) % sections,
            "cls": (((zh + dz) % nz) * nx + (xx + dx) % nx) * ny + (yy + dy) % ny,
        }

    zl, core = section // 2, section % 2

    def above(dz, low):
        return {"section": low * 2 + core, "cls": (((zh + dz) % nz) * nx + xx) * ny + yy}

    peers = [at(0, dx, 0, 0) for dx in range(1, nx)]
    peers += [at(0, 0, dy, 0) for dy in range(1, ny)]
    peers += [at(0, 0, 0, ds) for ds in range(1, sections)]
    peers += [above(1, 0), above(nz - 1, 1), above(2, 1 - zl)]
    barrier = pltpu.get_barrier_semaphore()
    for peer in peers:
        pl.semaphore_signal(barrier, inc=1, device_id=peer, device_id_type=MESH)

    inputs = {}
    for k, (src, dst) in enumerate(
        [
            (column_filters, colf),
            (row_filters, rowf),
            (basis_rows, bas.at[0]),
            (basis_columns, bas.at[1]),
            (mask, edge),
            (rotations, rot),
            (group_ids_hbm, group_ids),
            (references_hbm, references),
            (sharpness_hbm, sharpness),
            (best_rotation_hbm, best_rotation),
            (assignments_hbm, assignments),
        ]
    ):
        inputs[k] = pltpu.make_async_copy(src, dst, in_sem.at[k])
    for k in (2, 3, 6, 0):
        inputs[k].start()
    pltpu.make_async_copy(images.at[0], img.at[0], img_sem.at[0]).start()
    for k in (1, 4, 7):
        inputs[k].start()

    @pl.loop(1, particles)
    def _(n):
        pltpu.make_async_copy(images.at[n], img.at[n], img_sem.at[n]).start()

    for k in (8, 9, 10):
        inputs[k].start()
    inputs[5].start()

    inputs[2].wait()
    inputs[3].wait()
    row_at = lax.broadcasted_iota(jnp.int32, (nb, nb * nb), 0)
    lane_at = lax.broadcasted_iota(jnp.int32, (nb, nb * nb), 1)
    minor = (lane_at % nb == row_at).astype(jnp.float32).astype(jnp.bfloat16)
    major = (lane_at // nb == row_at).astype(jnp.float32).astype(jnp.bfloat16)
    tiled[...] = contract_first(bas[1], minor).astype(jnp.bfloat16)
    spread[...] = contract_first(bas[0], major)
    inputs[0].wait()
    inputs[1].wait()
    inputs[4].wait()
    inputs[6].wait()

    def filter_images(low, high, together):
        @pl.loop(low, high, step=together)
        def _(n):
            some = [n + k for k in range(together)]
            halves = []
            for m in some:
                pltpu.make_async_copy(images.at[m], img.at[m], img_sem.at[m]).wait()
                half = jnp.dot(img[m], colf[group_ids[m]], preferred_element_type=jnp.float32)
                halves.append(half.astype(jnp.bfloat16))
            masked = [
                jnp.dot(rowf[group_ids[m]], half, preferred_element_type=jnp.float32) * edge[...]
                for m, half in zip(some, halves)
            ]
            for m, one in zip(some, masked):
                squares[pl.ds(m, 1), :] = jnp.sum(one * one, axis=0, keepdims=True)
            inner = [jnp.dot(one.astype(jnp.bfloat16), tiled[...], preferred_element_type=jnp.float32) for one in masked]
            for m, one in zip(some, inner):
                raw[pl.ds(m, 1), :] = jnp.sum(one * spread[...], axis=0, keepdims=True)

    def send(k, src, dst, to):
        pltpu.make_async_remote_copy(
            src_ref=src,
            dst_ref=dst,
            send_sem=send_sem.at[k],
            recv_sem=recv_sem.at[k],
            device_id=to,
            device_id_type=MESH,
        ).start()

    def arrived(k, ref):
        pltpu.make_async_copy(ref, ref, recv_sem.at[k]).wait()

    def sent(k, ref):
        pltpu.make_async_copy(ref, ref, send_sem.at[k]).wait()

    filter_images(0, particles // 2, 4)

    pl.semaphore_wait(barrier, len(peers))
    inputs[7].wait()
    near[0] = references[...]
    for dy in range(1, ny):
        send(0, near.at[0], near.at[ny - dy], at(0, 0, dy, 0))
    for dx in range(1, nx):
        pl.semaphore_signal(ready, inc=1, device_id=at(0, dx, 0, 0), device_id_type=MESH)
    filter_images(particles // 2, particles, 4)

    eye = lax.broadcasted_iota(jnp.int32, (particles, particles), 0) == lax.broadcasted_iota(
        jnp.int32, (particles, particles), 1
    )
    inputs[8].wait()
    inputs[9].wait()
    sharp_row = sharpness[...].astype(jnp.float32)
    sharp = jnp.sum(jnp.where(eye, jnp.broadcast_to(sharp_row, (particles, particles)), 0.0), axis=1, keepdims=True)
    best_row = best_rotation[...].astype(jnp.float32)
    best = jnp.sum(jnp.where(eye, jnp.broadcast_to(best_row, (particles, particles)), 0.0), axis=1, keepdims=True)
    power = jnp.sum(squares[...], axis=1, keepdims=True) * (1.0 / (pix * pix))
    scale = lax.rsqrt(power + EPSILON) * sharp
    coef[0, :, 0:width] = (raw[...] * scale).astype(jnp.bfloat16)
    coef[0, :, width:] = jnp.broadcast_to(best, (particles, LANES)).astype(jnp.bfloat16)
    for ds in range(1, sections):
        send(2, coef.at[0], coef.at[sections - ds], at(0, 0, 0, ds))

    arrived(0, near.at[pl.ds(1, ny - 1)])
    refs[0] = jnp.concatenate([near[dy].astype(jnp.float32) for dy in range(ny)], axis=0).astype(jnp.bfloat16)
    pl.semaphore_wait(ready, nx - 1)
    side = 1 + (nz - 2) * zl
    for dx in (2, 1, 3, 0):
        if dx >= nx:
            continue
        for dz, low, slot in ((2, 1 - zl, 2), (2 * zl - 1 + nz, zl, side), (2 * zl - 1 + nz, 1 - zl, side), (0, zl, 0)):
            if dx or not isinstance(dz, int) or dz:
                to = {"section": low * 2 + core, "cls": (((zh + dz) % nz) * nx + (xx + dx) % nx) * ny + yy}
                send(1, refs.at[0], refs.at[(nx - dx) % nx * nz + slot], to)

    place = lax.broadcasted_iota(jnp.int32, (particles, classes), 1)
    dx_at, rest = place // (nz * ny * 2), place % (nz * ny * 2)
    dz_at, rest = rest // (ny * 2), rest % (ny * 2)
    dy_at, last = rest // 2, rest % 2
    name = ((((zh + dz_at) % nz) * nx + (xx + dx_at) % nx) * ny + (yy + dy_at) % ny) * 2 + last
    inputs[10].wait()
    listed = jnp.zeros((particles, classes), jnp.float32)
    for j in range(assignments.shape[1]):
        listed = jnp.where(assignments[:, j : j + 1] == name, 1.0, listed)

    place = lax.broadcasted_iota(jnp.int32, (classes, classes), 1)
    dx_at, rest = place // (ny * nz * 2), place % (ny * nz * 2)
    dy_at, rest = rest // (nz * 2), rest % (nz * 2)
    place = dx_at * (nz * ny * 2) + (rest // 2) * (ny * 2) + dy_at * 2 + rest % 2
    place = place == lax.broadcasted_iota(jnp.int32, (classes, classes), 0)
    reorder[...] = jnp.where(place, 1.0, 0.0).astype(jnp.bfloat16)

    inputs[5].wait()
    arrived(2, coef.at[pl.ds(1, sections - 1)])
    everyone = sections * particles
    gathered = coef[:, :, 0:width].reshape(everyone, width)
    best_all = coef[:, :, width:].astype(jnp.float32).reshape(everyone, LANES)
    best_all = jnp.concatenate([best_all] * (width // LANES), axis=1)
    first = (section * local).astype(jnp.float32)
    aligned = jnp.zeros((everyone, width), jnp.float32)
    for r in range(local):
        one = contract_last(gathered, rot[r])
        aligned = jnp.where(best_all == first + float(r), one, aligned)
        turned[pl.ds(r * everyone, everyone), :] = one.astype(jnp.bfloat16)
    turned_out[...] = aligned.astype(jnp.bfloat16).reshape(sections, particles, width)
    for ds in range(1, sections):
        send(3, turned_out.at[ds], turned_in.at[sections - ds], at(0, 0, 0, ds))

    arrived(3, turned_in.at[pl.ds(1, sections - 1)])
    mine = functools.reduce(
        jnp.add, [turned_out[0].astype(jnp.float32)] + [turned_in[d].astype(jnp.float32) for d in range(1, sections)]
    )
    mine = (mine * (1.0 / sharp)).astype(jnp.bfloat16)
    with_one = jnp.concatenate([mine, jnp.ones((particles, LANES), jnp.bfloat16)], axis=1)

    arrived(1, refs.at[pl.ds(1, nx * nz - 1)])
    all_refs = refs[...].reshape(classes, width)
    scores = contract_last(turned[...], all_refs).reshape(local, everyone, classes)
    largest = jnp.max(scores, axis=0)
    total = jnp.sum(jnp.exp(scores - largest), axis=0)
    marg_out[...] = (largest + jnp.log(total)).reshape(sections, particles, classes)
    for ds in range(1, sections):
        send(4, marg_out.at[ds], marg_in.at[sections - ds], at(0, 0, 0, ds))
    arrived(4, marg_in.at[pl.ds(1, sections - 1)])
    parts = [marg_out[0]] + [marg_in[d] for d in range(1, sections)]
    largest = functools.reduce(jnp.maximum, parts)
    marg = largest + jnp.log(functools.reduce(jnp.add, [jnp.exp(one - largest) for one in parts]))
    highest = jnp.max(jnp.where(listed > 0.0, marg, -jnp.inf), axis=1, keepdims=True)
    weight = jnp.where(listed > 0.0, jnp.exp(marg - highest), 0.0)
    weight = (weight / jnp.sum(weight, axis=1, keepdims=True)).astype(jnp.bfloat16)
    weight = jnp.dot(weight, reorder[...], preferred_element_type=jnp.float32).astype(jnp.bfloat16)
    sums = contract_first(weight, with_one)
    sum_y[...] = sums.reshape(sum_y.shape).astype(jnp.bfloat16)
    order = [(dx, dy) for dx in range(nx) for dy in range(ny) if (dx, dy) != (0, 0)]
    for dx, dy in sorted(order, key=lambda d: -min(d[0], nx - d[0]) - min(d[1], ny - d[1])):
        send(5, sum_y.at[dx * ny + dy], got_y.at[dx * ny + dy], at(0, dx, dy, 0))

    peak = jnp.max(marg, axis=1, keepdims=True)
    proof = peak + jnp.log(jnp.sum(jnp.exp(marg - peak), axis=1, keepdims=True))
    evidence[...] = jnp.sum(jnp.where(eye, jnp.broadcast_to(proof, (particles, particles)), 0.0), axis=0, keepdims=True)

    arrived(5, got_y.at[pl.ds(1, nx * ny - 1)])
    total = functools.reduce(
        jnp.add, [sum_y[0].astype(jnp.float32)] + [got_y[d].astype(jnp.float32) for d in range(1, nx * ny)]
    )
    for dz in range(nz):
        sum_z[dz] = total[2 * dz : 2 * dz + 2]
    for dz in range(nz):
        for ds in range(sections):
            if (dz, ds) != (0, 0):
                send(6, sum_z.at[dz], got_z.at[dz * sections + section], at(dz, 0, 0, ds))
    got_z[section] = sum_z[0]
    arrived(6, got_z.at[pl.ds(0, nz * sections - 1)])
    total = functools.reduce(jnp.add, [got_z[d] for d in range(nz * sections)])
    over = total[:, width:] + 1.0
    over = jnp.concatenate([over] * (width // LANES), axis=1)
    new_references[...] = (total[:, 0:width] + references[...].astype(jnp.float32)) / over

    sent(0, near.at[pl.ds(1, ny - 1)])
    sent(1, refs.at[pl.ds(1, nx * nz - 1)])
    sent(2, coef.at[pl.ds(1, sections - 1)])
    sent(3, turned_out.at[pl.ds(1, sections - 1)])
    sent(4, marg_out.at[pl.ds(1, sections - 1)])
    sent(5, sum_y.at[pl.ds(1, nx * ny - 1)])
    sent(6, got_z.at[pl.ds(0, nz * sections - 1)])


def hand_on(sums, proofs, new_references, evidence, sems):
    copies = [
        pltpu.make_async_copy(sums, new_references, sems.at[0]),
        pltpu.make_async_copy(proofs, evidence, sems.at[1]),
    ]
    for copy in copies:
        copy.start()
    for copy in copies:
        copy.wait()


def body(
    dims,
    images,
    group_ids,
    row_filters,
    column_filters,
    basis_rows,
    basis_columns,
    rotations,
    references,
    sharpness,
    best_rotation,
    assignments,
):
    nz, nx, ny = dims
    sections = 4
    particles, pix = images.shape[0], images.shape[1]
    nb = basis_rows.shape[1]
    local, width = rotations.shape[0], rotations.shape[1]
    classes = 2 * nz * nx * ny
    wide = width + LANES
    bf16, f32 = jnp.bfloat16, jnp.float32
    hbm = pl.BlockSpec(memory_space=pltpu.HBM)
    vmem = pl.BlockSpec(memory_space=pltpu.VMEM)
    new_references, evidence = pl.pallas_call(
        functools.partial(kernel, dims),
        out_shape=(
            jax.ShapeDtypeStruct((2, width), f32),
            jax.ShapeDtypeStruct((1, particles), f32),
        ),
        in_specs=[hbm] * 12,
        out_specs=(vmem, vmem),
        scratch_shapes=[
            pltpu.VMEM((particles, pix, pix), bf16),
            pltpu.VMEM(row_filters.shape, bf16),
            pltpu.VMEM(column_filters.shape, bf16),
            pltpu.VMEM((pix, pix), f32),
            pltpu.VMEM(rotations.shape, bf16),
            pltpu.VMEM((2, nb, pix), bf16),
            pltpu.VMEM((pix, nb * nb), bf16),
            pltpu.VMEM((pix, nb * nb), f32),
            pltpu.SMEM((particles,), jnp.int32),
            pltpu.VMEM((2, width), bf16),
            pltpu.VMEM((1, particles), bf16),
            pltpu.VMEM((1, particles), jnp.int32),
            pltpu.VMEM(assignments.shape, jnp.int32),
            pltpu.VMEM((particles, nb * nb), f32),
            pltpu.VMEM((particles, pix), f32),
            pltpu.VMEM((ny, 2, width), bf16),
            pltpu.VMEM((nx * nz, 2 * ny, width), bf16),
            pltpu.VMEM((classes, classes), bf16),
            pltpu.VMEM((sections, particles, wide), bf16),
            pltpu.VMEM((local * sections * particles, width), bf16),
            pltpu.VMEM((sections, particles, width), bf16),
            pltpu.VMEM((sections, particles, width), bf16),
            pltpu.VMEM((sections, particles, classes), f32),
            pltpu.VMEM((sections, particles, classes), f32),
            pltpu.VMEM((nx * ny, 2 * nz, wide), bf16),
            pltpu.VMEM((nx * ny, 2 * nz, wide), bf16),
            pltpu.VMEM((nz, 2, wide), f32),
            pltpu.VMEM((nz * sections, 2, wide), f32),
            pltpu.SemaphoreType.DMA((particles,)),
            pltpu.SemaphoreType.DMA((11,)),
            pltpu.SemaphoreType.DMA((7,)),
            pltpu.SemaphoreType.DMA((7,)),
            pltpu.SemaphoreType.REGULAR,
        ],
        compiler_params=pltpu.CompilerParams(
            collective_id=0, has_side_effects=True, vmem_limit_bytes=63 * 1024 * 1024
        ),
    )(
        images,
        group_ids,
        row_filters,
        column_filters,
        basis_rows.T,
        basis_columns.T,
        jnp.asarray(soft_edge(pix)),
        rotations,
        references,
        sharpness.reshape(1, particles),
        best_rotation.reshape(1, particles),
        assignments,
    )
    new_references, evidence = pl.pallas_call(
        hand_on,
        out_shape=(
            jax.ShapeDtypeStruct((2, width), f32),
            jax.ShapeDtypeStruct((1, particles), f32),
        ),
        in_specs=[hbm, hbm],
        out_specs=(hbm, hbm),
        scratch_shapes=[pltpu.SemaphoreType.DMA((2,))],
    )(new_references, evidence)
    return new_references, evidence.reshape(particles)


def solution(mesh, dims=TORUS):
    in_specs = (
        P(("section", "cls"), None, None),
        P(("section", "cls")),
        P(),
        P(),
        P(),
        P(),
        P("section", None, None),
        P("cls", None),
        P(("section", "cls")),
        P(("section", "cls")),
        P(("section", "cls"), None),
    )
    out_specs = (P("cls", None), P(("section", "cls")))
    return jax.shard_map(
        functools.partial(body, dims), mesh=mesh, in_specs=in_specs, out_specs=out_specs, check_vma=False
    )
```

```python
import functools
import math

import jax
import jax.numpy as jnp
import numpy as np
from jax import lax
from jax.experimental import pallas as pl
from jax.experimental.pallas import tpu as pltpu
from jax.sharding import PartitionSpec as P

EPSILON = 1e-05
TORUS = (4, 4, 8)
MESH = pl.DeviceIdType.MESH
LANES = 128


def soft_edge(pixels):
    coordinate = (np.arange(pixels, dtype=np.float32) - np.float32((pixels - 1) / 2.0)) / np.float32(pixels / 2.0)
    radius = np.sqrt(coordinate[:, None] * coordinate[:, None] + coordinate[None, :] * coordinate[None, :])
    falloff = np.clip((radius - np.float32(0.8)) / np.float32(0.15), 0.0, 1.0)
    return (0.5 + 0.5 * np.cos(math.pi * falloff)).astype(np.float32)


def contract_last(a, b):
    return lax.dot_general(a, b, (((1,), (1,)), ((), ())), preferred_element_type=jnp.float32)


def contract_first(a, b):
    return lax.dot_general(a, b, (((0,), (0,)), ((), ())), preferred_element_type=jnp.float32)


def kernel(
    dims,
    images,
    group_ids_hbm,
    row_filters,
    column_filters,
    basis_rows,
    basis_columns,
    mask,
    rotations,
    references_hbm,
    sharpness_hbm,
    best_rotation_hbm,
    assignments_hbm,
    new_references,
    evidence,
    img,
    rowf,
    colf,
    edge,
    rot,
    bas,
    tiled,
    spread,
    group_ids,
    references,
    sharpness,
    best_rotation,
    assignments,
    raw,
    squares,
    near,
    refs,
    reorder,
    coef,
    turned,
    turned_out,
    turned_in,
    marg_out,
    marg_in,
    sum_y,
    got_y,
    sum_z,
    got_z,
    img_sem,
    in_sem,
    send_sem,
    recv_sem,
    ready,
):
    nz, nx, ny = dims
    section, cls = lax.axis_index("section"), lax.axis_index("cls")
    sections = 4
    zh = cls // (nx * ny)
    xx = (cls // ny) % nx
    yy = cls % ny
    particles, pix = img.shape[0], img.shape[1]
    local = rot.shape[0]
    width = rot.shape[1]
    classes = nz * nx * ny * 2
    nb = bas.shape[1]

    def at(dz, dx, dy, ds):
        return {
            "section": (section + ds) % sections,
            "cls": (((zh + dz) % nz) * nx + (xx + dx) % nx) * ny + (yy + dy) % ny,
        }

    zl, core = section // 2, section % 2

    def above(dz, low):
        return {"section": low * 2 + core, "cls": (((zh + dz) % nz) * nx + xx) * ny + yy}

    peers = [at(0, dx, 0, 0) for dx in range(1, nx)]
    peers += [at(0, 0, dy, 0) for dy in range(1, ny)]
    peers += [at(0, 0, 0, ds) for ds in range(1, sections)]
    peers += [above(1, 0), above(nz - 1, 1), above(2, 1 - zl)]
    barrier = pltpu.get_barrier_semaphore()
    for peer in peers:
        pl.semaphore_signal(barrier, inc=1, device_id=peer, device_id_type=MESH)

    inputs = {}
    for k, (src, dst) in enumerate(
        [
            (column_filters, colf),
            (row_filters, rowf),
            (basis_rows, bas.at[0]),
            (basis_columns, bas.at[1]),
            (mask, edge),
            (rotations, rot),
            (group_ids_hbm, group_ids),
            (references_hbm, references),
            (sharpness_hbm, sharpness),
            (best_rotation_hbm, best_rotation),
            (assignments_hbm, assignments),
        ]
    ):
        inputs[k] = pltpu.make_async_copy(src, dst, in_sem.at[k])
    for k in (2, 3, 6, 0):
        inputs[k].start()
    pltpu.make_async_copy(images.at[0], img.at[0], img_sem.at[0]).start()
    for k in (1, 4, 7):
        inputs[k].start()

    @pl.loop(1, particles)
    def _(n):
        pltpu.make_async_copy(images.at[n], img.at[n], img_sem.at[n]).start()

    for k in (8, 9, 10):
        inputs[k].start()
    inputs[5].start()

    inputs[2].wait()
    inputs[3].wait()
    row_at = lax.broadcasted_iota(jnp.int32, (nb, nb * nb), 0)
    lane_at = lax.broadcasted_iota(jnp.int32, (nb, nb * nb), 1)
    minor = (lane_at % nb == row_at).astype(jnp.float32).astype(jnp.bfloat16)
    major = (lane_at // nb == row_at).astype(jnp.float32).astype(jnp.bfloat16)
    tiled[...] = contract_first(bas[1], minor).astype(jnp.bfloat16)
    spread[...] = contract_first(bas[0], major)
    inputs[0].wait()
    inputs[1].wait()
    inputs[4].wait()
    inputs[6].wait()

    def filter_images(low, high, together):
        @pl.loop(low, high, step=together)
        def _(n):
            some = [n + k for k in range(together)]
            halves = []
            for m in some:
                pltpu.make_async_copy(images.at[m], img.at[m], img_sem.at[m]).wait()
                half = jnp.dot(img[m], colf[group_ids[m]], preferred_element_type=jnp.float32)
                halves.append(half.astype(jnp.bfloat16))
            masked = [
                jnp.dot(rowf[group_ids[m]], half, preferred_element_type=jnp.float32) * edge[...]
                for m, half in zip(some, halves)
            ]
            for m, one in zip(some, masked):
                squares[pl.ds(m, 1), :] = jnp.sum(one * one, axis=0, keepdims=True)
            inner = [jnp.dot(one.astype(jnp.bfloat16), tiled[...], preferred_element_type=jnp.float32) for one in masked]
            for m, one in zip(some, inner):
                raw[pl.ds(m, 1), :] = jnp.sum(one * spread[...], axis=0, keepdims=True)

    def send(k, src, dst, to):
        pltpu.make_async_remote_copy(
            src_ref=src,
            dst_ref=dst,
            send_sem=send_sem.at[k],
            recv_sem=recv_sem.at[k],
            device_id=to,
            device_id_type=MESH,
        ).start()

    def arrived(k, ref):
        pltpu.make_async_copy(ref, ref, recv_sem.at[k]).wait()

    def sent(k, ref):
        pltpu.make_async_copy(ref, ref, send_sem.at[k]).wait()

    filter_images(0, particles // 2, 4)

    pl.semaphore_wait(barrier, len(peers))
    inputs[7].wait()
    near[0] = references[...]
    for dy in range(1, ny):
        send(0, near.at[0], near.at[ny - dy], at(0, 0, dy, 0))
    for dx in range(1, nx):
        pl.semaphore_signal(ready, inc=1, device_id=at(0, dx, 0, 0), device_id_type=MESH)
    filter_images(particles // 2, particles, 4)

    eye = lax.broadcasted_iota(jnp.int32, (particles, particles), 0) == lax.broadcasted_iota(
        jnp.int32, (particles, particles), 1
    )
    inputs[8].wait()
    inputs[9].wait()
    sharp_row = sharpness[...].astype(jnp.float32)
    sharp = jnp.sum(jnp.where(eye, jnp.broadcast_to(sharp_row, (particles, particles)), 0.0), axis=1, keepdims=True)
    best_row = best_rotation[...].astype(jnp.float32)
    best = jnp.sum(jnp.where(eye, jnp.broadcast_to(best_row, (particles, particles)), 0.0), axis=1, keepdims=True)
    power = jnp.sum(squares[...], axis=1, keepdims=True) * (1.0 / (pix * pix))
    scale = lax.rsqrt(power + EPSILON) * sharp
    coef[0, :, 0:width] = (raw[...] * scale).astype(jnp.bfloat16)
    coef[0, :, width:] = jnp.broadcast_to(best, (particles, LANES)).astype(jnp.bfloat16)
    for ds in range(1, sections):
        send(2, coef.at[0], coef.at[sections - ds], at(0, 0, 0, ds))

    arrived(0, near.at[pl.ds(1, ny - 1)])
    refs[0] = jnp.concatenate([near[dy].astype(jnp.float32) for dy in range(ny)], axis=0).astype(jnp.bfloat16)
    pl.semaphore_wait(ready, nx - 1)
    side = 1 + (nz - 2) * zl
    for dx in (2, 1, 3, 0):
        if dx >= nx:
            continue
        for dz, low, slot in ((2, 1 - zl, 2), (2 * zl - 1 + nz, zl, side), (2 * zl - 1 + nz, 1 - zl, side), (0, zl, 0)):
            if dx or not isinstance(dz, int) or dz:
                to = {"section": low * 2 + core, "cls": (((zh + dz) % nz) * nx + (xx + dx) % nx) * ny + yy}
                send(1, refs.at[0], refs.at[(nx - dx) % nx * nz + slot], to)

    place = lax.broadcasted_iota(jnp.int32, (particles, classes), 1)
    dx_at, rest = place // (nz * ny * 2), place % (nz * ny * 2)
    dz_at, rest = rest // (ny * 2), rest % (ny * 2)
    dy_at, last = rest // 2, rest % 2
    name = ((((zh + dz_at) % nz) * nx + (xx + dx_at) % nx) * ny + (yy + dy_at) % ny) * 2 + last
    inputs[10].wait()
    listed = jnp.zeros((particles, classes), jnp.float32)
    for j in range(assignments.shape[1]):
        listed = jnp.where(assignments[:, j : j + 1] == name, 1.0, listed)

    place = lax.broadcasted_iota(jnp.int32, (classes, classes), 1)
    dx_at, rest = place // (ny * nz * 2), place % (ny * nz * 2)
    dy_at, rest = rest // (nz * 2), rest % (nz * 2)
    place = dx_at * (nz * ny * 2) + (rest // 2) * (ny * 2) + dy_at * 2 + rest % 2
    place = place == lax.broadcasted_iota(jnp.int32, (classes, classes), 0)
    reorder[...] = jnp.where(place, 1.0, 0.0).astype(jnp.bfloat16)

    inputs[5].wait()
    arrived(2, coef.at[pl.ds(1, sections - 1)])
    everyone = sections * particles
    gathered = coef[:, :, 0:width].reshape(everyone, width)
    best_all = coef[:, :, width:].astype(jnp.float32).reshape(everyone, LANES)
    best_all = jnp.concatenate([best_all] * (width // LANES), axis=1)
    first = (section * local).astype(jnp.float32)
    aligned = jnp.zeros((everyone, width), jnp.float32)
    for r in range(local):
        one = contract_last(gathered, rot[r])
        aligned = jnp.where(best_all == first + float(r), one, aligned)
        turned[pl.ds(r * everyone, everyone), :] = one.astype(jnp.bfloat16)
    turned_out[...] = aligned.astype(jnp.bfloat16).reshape(sections, particles, width)
    for ds in range(1, sections):
        send(3, turned_out.at[ds], turned_in.at[sections - ds], at(0, 0, 0, ds))

    arrived(3, turned_in.at[pl.ds(1, sections - 1)])
    mine = functools.reduce(
        jnp.add, [turned_out[0].astype(jnp.float32)] + [turned_in[d].astype(jnp.float32) for d in range(1, sections)]
    )
    mine = (mine * (1.0 / sharp)).astype(jnp.bfloat16)
    with_one = jnp.concatenate([mine, jnp.ones((particles, LANES), jnp.bfloat16)], axis=1)

    arrived(1, refs.at[pl.ds(1, nx * nz - 1)])
    all_refs = refs[...].reshape(classes, width)
    scores = contract_last(turned[...], all_refs).reshape(local, everyone, classes)
    largest = jnp.max(scores, axis=0)
    total = jnp.sum(jnp.exp(scores - largest), axis=0)
    marg_out[...] = (largest + jnp.log(total)).reshape(sections, particles, classes)
    for ds in range(1, sections):
        send(4, marg_out.at[ds], marg_in.at[sections - ds], at(0, 0, 0, ds))
    arrived(4, marg_in.at[pl.ds(1, sections - 1)])
    parts = [marg_out[0]] + [marg_in[d] for d in range(1, sections)]
    largest = functools.reduce(jnp.maximum, parts)
    marg = largest + jnp.log(functools.reduce(jnp.add, [jnp.exp(one - largest) for one in parts]))
    highest = jnp.max(jnp.where(listed > 0.0, marg, -jnp.inf), axis=1, keepdims=True)
    weight = jnp.where(listed > 0.0, jnp.exp(marg - highest), 0.0)
    weight = (weight / jnp.sum(weight, axis=1, keepdims=True)).astype(jnp.bfloat16)
    weight = jnp.dot(weight, reorder[...], preferred_element_type=jnp.float32).astype(jnp.bfloat16)
    sums = contract_first(weight, with_one)
    sum_y[...] = sums.reshape(sum_y.shape).astype(jnp.bfloat16)
    order = [(dx, dy) for dx in range(nx) for dy in range(ny) if (dx, dy) != (0, 0)]
    for dx, dy in sorted(order, key=lambda d: -min(d[0], nx - d[0]) - min(d[1], ny - d[1])):
        send(5, sum_y.at[dx * ny + dy], got_y.at[dx * ny + dy], at(0, dx, dy, 0))

    peak = jnp.max(marg, axis=1, keepdims=True)
    proof = peak + jnp.log(jnp.sum(jnp.exp(marg - peak), axis=1, keepdims=True))
    evidence[...] = jnp.sum(jnp.where(eye, jnp.broadcast_to(proof, (particles, particles)), 0.0), axis=0, keepdims=True)

    arrived(5, got_y.at[pl.ds(1, nx * ny - 1)])
    total = functools.reduce(
        jnp.add, [sum_y[0].astype(jnp.float32)] + [got_y[d].astype(jnp.float32) for d in range(1, nx * ny)]
    )
    for dz in range(nz):
        sum_z[dz] = total[2 * dz : 2 * dz + 2]
    for dz in range(nz):
        for ds in range(sections):
            if (dz, ds) != (0, 0):
                send(6, sum_z.at[dz], got_z.at[dz * sections + section], at(dz, 0, 0, ds))
    got_z[section] = sum_z[0]
    arrived(6, got_z.at[pl.ds(0, nz * sections - 1)])
    total = functools.reduce(jnp.add, [got_z[d] for d in range(nz * sections)])
    over = total[:, width:] + 1.0
    over = jnp.concatenate([over] * (width // LANES), axis=1)
    new_references[...] = (total[:, 0:width] + references[...].astype(jnp.float32)) / over

    sent(0, near.at[pl.ds(1, ny - 1)])
    sent(1, refs.at[pl.ds(1, nx * nz - 1)])
    sent(2, coef.at[pl.ds(1, sections - 1)])
    sent(3, turned_out.at[pl.ds(1, sections - 1)])
    sent(4, marg_out.at[pl.ds(1, sections - 1)])
    sent(5, sum_y.at[pl.ds(1, nx * ny - 1)])
    sent(6, got_z.at[pl.ds(0, nz * sections - 1)])


def hand_on(sums, proofs, new_references, evidence, sems):
    copies = [
        pltpu.make_async_copy(sums, new_references, sems.at[0]),
        pltpu.make_async_copy(proofs, evidence, sems.at[1]),
    ]
    for copy in copies:
        copy.start()
    for copy in copies:
        copy.wait()


def body(
    dims,
    images,
    group_ids,
    row_filters,
    column_filters,
    basis_rows,
    basis_columns,
    rotations,
    references,
    sharpness,
    best_rotation,
    assignments,
):
    nz, nx, ny = dims
    sections = 4
    particles, pix = images.shape[0], images.shape[1]
    nb = basis_rows.shape[1]
    local, width = rotations.shape[0], rotations.shape[1]
    classes = 2 * nz * nx * ny
    wide = width + LANES
    bf16, f32 = jnp.bfloat16, jnp.float32
    hbm = pl.BlockSpec(memory_space=pltpu.HBM)
    vmem = pl.BlockSpec(memory_space=pltpu.VMEM)
    new_references, evidence = pl.pallas_call(
        functools.partial(kernel, dims),
        out_shape=(
            pltpu.VMEM((2, width), f32),
            pltpu.VMEM((1, particles), f32),
        ),
        in_specs=[hbm] * 12,
        out_specs=(vmem, vmem),
        scratch_shapes=[
            pltpu.VMEM((particles, pix, pix), bf16),
            pltpu.VMEM(row_filters.shape, bf16),
            pltpu.VMEM(column_filters.shape, bf16),
            pltpu.VMEM((pix, pix), f32),
            pltpu.VMEM(rotations.shape, bf16),
            pltpu.VMEM((2, nb, pix), bf16),
            pltpu.VMEM((pix, nb * nb), bf16),
            pltpu.VMEM((pix, nb * nb), f32),
            pltpu.SMEM((particles,), jnp.int32),
            pltpu.VMEM((2, width), bf16),
            pltpu.VMEM((1, particles), bf16),
            pltpu.VMEM((1, particles), jnp.int32),
            pltpu.VMEM(assignments.shape, jnp.int32),
            pltpu.VMEM((particles, nb * nb), f32),
            pltpu.VMEM((particles, pix), f32),
            pltpu.VMEM((ny, 2, width), bf16),
            pltpu.VMEM((nx * nz, 2 * ny, width), bf16),
            pltpu.VMEM((classes, classes), bf16),
            pltpu.VMEM((sections, particles, wide), bf16),
            pltpu.VMEM((local * sections * particles, width), bf16),
            pltpu.VMEM((sections, particles, width), bf16),
            pltpu.VMEM((sections, particles, width), bf16),
            pltpu.VMEM((sections, particles, classes), f32),
            pltpu.VMEM((sections, particles, classes), f32),
            pltpu.VMEM((nx * ny, 2 * nz, wide), bf16),
            pltpu.VMEM((nx * ny, 2 * nz, wide), bf16),
            pltpu.VMEM((nz, 2, wide), f32),
            pltpu.VMEM((nz * sections, 2, wide), f32),
            pltpu.SemaphoreType.DMA((particles,)),
            pltpu.SemaphoreType.DMA((11,)),
            pltpu.SemaphoreType.DMA((7,)),
            pltpu.SemaphoreType.DMA((7,)),
            pltpu.SemaphoreType.REGULAR,
        ],
        compiler_params=pltpu.CompilerParams(
            collective_id=0, has_side_effects=True, vmem_limit_bytes=63 * 1024 * 1024
        ),
    )(
        images,
        group_ids,
        row_filters,
        column_filters,
        basis_rows.T,
        basis_columns.T,
        jnp.asarray(soft_edge(pix)),
        rotations,
        references,
        sharpness.reshape(1, particles),
        best_rotation.reshape(1, particles),
        assignments,
    )
    new_references, evidence = pl.pallas_call(
        hand_on,
        out_shape=(
            jax.ShapeDtypeStruct((2, width), f32),
            jax.ShapeDtypeStruct((1, particles), f32),
        ),
        in_specs=[vmem, vmem],
        out_specs=(hbm, hbm),
        scratch_shapes=[pltpu.SemaphoreType.DMA((2,))],
        compiler_params=pltpu.CompilerParams(vmem_limit_bytes=1024 * 1024),
    )(new_references, evidence)
    return new_references, evidence.reshape(particles)


def solution(mesh, dims=TORUS):
    in_specs = (
        P(("section", "cls"), None, None),
        P(("section", "cls")),
        P(),
        P(),
        P(),
        P(),
        P("section", None, None),
        P("cls", None),
        P(("section", "cls")),
        P(("section", "cls")),
        P(("section", "cls"), None),
    )
    out_specs = (P("cls", None), P(("section", "cls")))
    return jax.shard_map(
        functools.partial(body, dims), mesh=mesh, in_specs=in_specs, out_specs=out_specs, check_vma=False
    )
```

```python
import functools
import math

import jax
import jax.numpy as jnp
import numpy as np
from jax import lax
from jax.experimental import pallas as pl
from jax.experimental.pallas import tpu as pltpu
from jax.sharding import PartitionSpec as P

EPSILON = 1e-05
TORUS = (4, 4, 8)
MESH = pl.DeviceIdType.MESH
LANES = 128


def soft_edge(pixels):
    coordinate = (np.arange(pixels, dtype=np.float32) - np.float32((pixels - 1) / 2.0)) / np.float32(pixels / 2.0)
    radius = np.sqrt(coordinate[:, None] * coordinate[:, None] + coordinate[None, :] * coordinate[None, :])
    falloff = np.clip((radius - np.float32(0.8)) / np.float32(0.15), 0.0, 1.0)
    return (0.5 + 0.5 * np.cos(math.pi * falloff)).astype(np.float32)


def contract_last(a, b):
    return lax.dot_general(a, b, (((1,), (1,)), ((), ())), preferred_element_type=jnp.float32)


def contract_first(a, b):
    return lax.dot_general(a, b, (((0,), (0,)), ((), ())), preferred_element_type=jnp.float32)


def kernel(
    dims,
    images,
    group_ids_hbm,
    row_filters,
    column_filters,
    basis_rows,
    basis_columns,
    mask,
    rotations,
    references_hbm,
    sharpness_hbm,
    best_rotation_hbm,
    assignments_hbm,
    new_references,
    evidence,
    img,
    rowf,
    colf,
    edge,
    rot,
    bas,
    tiled,
    spread,
    group_ids,
    references,
    sharpness,
    best_rotation,
    assignments,
    raw,
    squares,
    near,
    refs,
    reorder,
    coef,
    turned,
    turned_out,
    turned_in,
    marg_out,
    marg_in,
    sum_y,
    got_y,
    sum_z,
    got_z,
    img_sem,
    in_sem,
    send_sem,
    recv_sem,
    ready,
):
    nz, nx, ny = dims
    section, cls = lax.axis_index("section"), lax.axis_index("cls")
    sections = 4
    zh = cls // (nx * ny)
    xx = (cls // ny) % nx
    yy = cls % ny
    particles, pix = img.shape[0], img.shape[1]
    local = rot.shape[0]
    width = rot.shape[1]
    classes = nz * nx * ny * 2
    nb = bas.shape[1]

    def at(dz, dx, dy, ds):
        return {
            "section": (section + ds) % sections,
            "cls": (((zh + dz) % nz) * nx + (xx + dx) % nx) * ny + (yy + dy) % ny,
        }

    zl, core = section // 2, section % 2

    def above(dz, low):
        return {"section": low * 2 + core, "cls": (((zh + dz) % nz) * nx + xx) * ny + yy}

    along_y = sorted(range(1, ny), key=lambda d: -min(d, ny - d))
    along_x = sorted(range(1, nx), key=lambda d: -min(d, nx - d))
    along_z = sorted(range(nz), key=lambda d: -min(d, nz - d))
    inside = (2, 1, 3)
    peers = [at(0, 0, dy, 0) for dy in along_y]
    peers += [above(2, 1 - zl), above(1, 0), above(nz - 1, 1)]
    peers += [at(0, dx, 0, 0) for dx in along_x]
    peers += [at(0, 0, 0, ds) for ds in inside]
    barrier = pltpu.get_barrier_semaphore()
    for peer in peers:
        pl.semaphore_signal(barrier, inc=1, device_id=peer, device_id_type=MESH)

    inputs = {}
    for k, (src, dst) in enumerate(
        [
            (column_filters, colf),
            (row_filters, rowf),
            (basis_rows, bas.at[0]),
            (basis_columns, bas.at[1]),
            (mask, edge),
            (rotations, rot),
            (group_ids_hbm, group_ids),
            (references_hbm, references),
            (sharpness_hbm, sharpness),
            (best_rotation_hbm, best_rotation),
            (assignments_hbm, assignments),
        ]
    ):
        inputs[k] = pltpu.make_async_copy(src, dst, in_sem.at[k])
    for k in (2, 3, 6, 0):
        inputs[k].start()
    pltpu.make_async_copy(images.at[0], img.at[0], img_sem.at[0]).start()
    for k in (1, 4, 7):
        inputs[k].start()

    @pl.loop(1, particles)
    def _(n):
        pltpu.make_async_copy(images.at[n], img.at[n], img_sem.at[n]).start()

    for k in (8, 9, 10):
        inputs[k].start()
    inputs[5].start()

    inputs[2].wait()
    inputs[3].wait()
    row_at = lax.broadcasted_iota(jnp.int32, (nb, nb * nb), 0)
    lane_at = lax.broadcasted_iota(jnp.int32, (nb, nb * nb), 1)
    minor = (lane_at % nb == row_at).astype(jnp.float32).astype(jnp.bfloat16)
    major = (lane_at // nb == row_at).astype(jnp.float32).astype(jnp.bfloat16)
    tiled[...] = contract_first(bas[1], minor).astype(jnp.bfloat16)
    spread[...] = contract_first(bas[0], major)
    inputs[0].wait()
    inputs[1].wait()
    inputs[4].wait()
    inputs[6].wait()

    def filter_images(low, high, together):
        @pl.loop(low, high, step=together)
        def _(n):
            some = [n + k for k in range(together)]
            halves = []
            for m in some:
                pltpu.make_async_copy(images.at[m], img.at[m], img_sem.at[m]).wait()
                half = jnp.dot(img[m], colf[group_ids[m]], preferred_element_type=jnp.float32)
                halves.append(half.astype(jnp.bfloat16))
            masked = [
                jnp.dot(rowf[group_ids[m]], half, preferred_element_type=jnp.float32) * edge[...]
                for m, half in zip(some, halves)
            ]
            for m, one in zip(some, masked):
                squares[pl.ds(m, 1), :] = jnp.sum(one * one, axis=0, keepdims=True)
            inner = [jnp.dot(one.astype(jnp.bfloat16), tiled[...], preferred_element_type=jnp.float32) for one in masked]
            for m, one in zip(some, inner):
                raw[pl.ds(m, 1), :] = jnp.sum(one * spread[...], axis=0, keepdims=True)

    def send(k, src, dst, to):
        pltpu.make_async_remote_copy(
            src_ref=src,
            dst_ref=dst,
            send_sem=send_sem.at[k],
            recv_sem=recv_sem.at[k],
            device_id=to,
            device_id_type=MESH,
        ).start()

    def arrived(k, ref):
        pltpu.make_async_copy(ref, ref, recv_sem.at[k]).wait()

    def sent(k, ref):
        pltpu.make_async_copy(ref, ref, send_sem.at[k]).wait()

    filter_images(0, particles // 4, 4)

    pl.semaphore_wait(barrier, len(peers))
    inputs[7].wait()
    near[0] = references[...]
    for dy in along_y:
        send(0, near.at[0], near.at[ny - dy], at(0, 0, dy, 0))
    for dx in along_x:
        pl.semaphore_signal(ready, inc=1, device_id=at(0, dx, 0, 0), device_id_type=MESH)
    filter_images(particles // 4, particles, 4)

    eye = lax.broadcasted_iota(jnp.int32, (particles, particles), 0) == lax.broadcasted_iota(
        jnp.int32, (particles, particles), 1
    )
    inputs[8].wait()
    inputs[9].wait()
    sharp_row = sharpness[...].astype(jnp.float32)
    sharp = jnp.sum(jnp.where(eye, jnp.broadcast_to(sharp_row, (particles, particles)), 0.0), axis=1, keepdims=True)
    best_row = best_rotation[...].astype(jnp.float32)
    best = jnp.sum(jnp.where(eye, jnp.broadcast_to(best_row, (particles, particles)), 0.0), axis=1, keepdims=True)
    power = jnp.sum(squares[...], axis=1, keepdims=True) * (1.0 / (pix * pix))
    scale = lax.rsqrt(power + EPSILON) * sharp
    coef[0, :, 0:width] = (raw[...] * scale).astype(jnp.bfloat16)
    coef[0, :, width:] = jnp.broadcast_to(best, (particles, LANES)).astype(jnp.bfloat16)
    for ds in inside:
        send(2, coef.at[0], coef.at[sections - ds], at(0, 0, 0, ds))

    arrived(0, near.at[pl.ds(1, ny - 1)])
    refs[0] = jnp.concatenate([near[dy].astype(jnp.float32) for dy in range(ny)], axis=0).astype(jnp.bfloat16)
    pl.semaphore_wait(ready, nx - 1)
    side = 1 + (nz - 2) * zl
    for dx in (2, 1, 3, 0):
        if dx >= nx:
            continue
        for dz, low, slot in ((2, 1 - zl, 2), (2 * zl - 1 + nz, zl, side), (2 * zl - 1 + nz, 1 - zl, side), (0, zl, 0)):
            if dx or not isinstance(dz, int) or dz:
                to = {"section": low * 2 + core, "cls": (((zh + dz) % nz) * nx + (xx + dx) % nx) * ny + yy}
                send(1, refs.at[0], refs.at[(nx - dx) % nx * nz + slot], to)

    place = lax.broadcasted_iota(jnp.int32, (particles, classes), 1)
    dx_at, rest = place // (nz * ny * 2), place % (nz * ny * 2)
    dz_at, rest = rest // (ny * 2), rest % (ny * 2)
    dy_at, last = rest // 2, rest % 2
    name = ((((zh + dz_at) % nz) * nx + (xx + dx_at) % nx) * ny + (yy + dy_at) % ny) * 2 + last
    inputs[10].wait()
    listed = jnp.zeros((particles, classes), jnp.float32)
    for j in range(assignments.shape[1]):
        listed = jnp.where(assignments[:, j : j + 1] == name, 1.0, listed)

    place = lax.broadcasted_iota(jnp.int32, (classes, classes), 1)
    dx_at, rest = place // (ny * nz * 2), place % (ny * nz * 2)
    dy_at, rest = rest // (nz * 2), rest % (nz * 2)
    place = dx_at * (nz * ny * 2) + (rest // 2) * (ny * 2) + dy_at * 2 + rest % 2
    place = place == lax.broadcasted_iota(jnp.int32, (classes, classes), 0)
    reorder[...] = jnp.where(place, 1.0, 0.0).astype(jnp.bfloat16)

    inputs[5].wait()
    arrived(2, coef.at[pl.ds(1, sections - 1)])
    everyone = sections * particles
    gathered = coef[:, :, 0:width].reshape(everyone, width)
    best_all = coef[:, :, width:].astype(jnp.float32).reshape(everyone, LANES)
    best_all = jnp.concatenate([best_all] * (width // LANES), axis=1)
    first = (section * local).astype(jnp.float32)
    aligned = jnp.zeros((everyone, width), jnp.float32)
    for r in range(local):
        one = contract_last(gathered, rot[r])
        aligned = jnp.where(best_all == first + float(r), one, aligned)
        turned[pl.ds(r * everyone, everyone), :] = one.astype(jnp.bfloat16)
    turned_out[...] = aligned.astype(jnp.bfloat16).reshape(sections, particles, width)
    for ds in inside:
        send(3, turned_out.at[ds], turned_in.at[sections - ds], at(0, 0, 0, ds))

    arrived(3, turned_in.at[pl.ds(1, sections - 1)])
    mine = functools.reduce(
        jnp.add, [turned_out[0].astype(jnp.float32)] + [turned_in[d].astype(jnp.float32) for d in range(1, sections)]
    )
    mine = (mine * (1.0 / sharp)).astype(jnp.bfloat16)
    with_one = jnp.concatenate([mine, jnp.ones((particles, LANES), jnp.bfloat16)], axis=1)

    arrived(1, refs.at[pl.ds(1, nx * nz - 1)])
    all_refs = refs[...].reshape(classes, width)
    scores = contract_last(turned[...], all_refs).reshape(local, everyone, classes)
    largest = jnp.max(scores, axis=0)
    total = jnp.sum(jnp.exp(scores - largest), axis=0)
    marg_out[...] = (largest + jnp.log(total)).reshape(sections, particles, classes)
    for ds in inside:
        send(4, marg_out.at[ds], marg_in.at[sections - ds], at(0, 0, 0, ds))
    arrived(4, marg_in.at[pl.ds(1, sections - 1)])
    parts = [marg_out[0]] + [marg_in[d] for d in range(1, sections)]
    largest = functools.reduce(jnp.maximum, parts)
    marg = largest + jnp.log(functools.reduce(jnp.add, [jnp.exp(one - largest) for one in parts]))
    highest = jnp.max(jnp.where(listed > 0.0, marg, -jnp.inf), axis=1, keepdims=True)
    weight = jnp.where(listed > 0.0, jnp.exp(marg - highest), 0.0)
    weight = (weight / jnp.sum(weight, axis=1, keepdims=True)).astype(jnp.bfloat16)
    weight = jnp.dot(weight, reorder[...], preferred_element_type=jnp.float32).astype(jnp.bfloat16)
    sums = contract_first(weight, with_one)
    sum_y[...] = sums.reshape(sum_y.shape).astype(jnp.bfloat16)
    order = [(dx, dy) for dx in range(nx) for dy in range(ny) if (dx, dy) != (0, 0)]
    for dx, dy in sorted(order, key=lambda d: -min(d[0], nx - d[0]) - min(d[1], ny - d[1])):
        send(5, sum_y.at[dx * ny + dy], got_y.at[dx * ny + dy], at(0, dx, dy, 0))

    peak = jnp.max(marg, axis=1, keepdims=True)
    proof = peak + jnp.log(jnp.sum(jnp.exp(marg - peak), axis=1, keepdims=True))
    evidence[...] = jnp.sum(jnp.where(eye, jnp.broadcast_to(proof, (particles, particles)), 0.0), axis=0, keepdims=True)

    arrived(5, got_y.at[pl.ds(1, nx * ny - 1)])
    total = functools.reduce(
        jnp.add, [sum_y[0].astype(jnp.float32)] + [got_y[d].astype(jnp.float32) for d in range(1, nx * ny)]
    )
    for dz in range(nz):
        sum_z[dz] = total[2 * dz : 2 * dz + 2]
    for dz in along_z:
        for ds in (*inside, 0):
            if (dz, ds) != (0, 0):
                send(6, sum_z.at[dz], got_z.at[dz * sections + section], at(dz, 0, 0, ds))
    got_z[section] = sum_z[0]
    arrived(6, got_z.at[pl.ds(0, nz * sections - 1)])
    total = functools.reduce(jnp.add, [got_z[d] for d in range(nz * sections)])
    over = total[:, width:] + 1.0
    over = jnp.concatenate([over] * (width // LANES), axis=1)
    new_references[...] = (total[:, 0:width] + references[...].astype(jnp.float32)) / over

    sent(0, near.at[pl.ds(1, ny - 1)])
    sent(1, refs.at[pl.ds(1, nx * nz - 1)])
    sent(2, coef.at[pl.ds(1, sections - 1)])
    sent(3, turned_out.at[pl.ds(1, sections - 1)])
    sent(4, marg_out.at[pl.ds(1, sections - 1)])
    sent(5, sum_y.at[pl.ds(1, nx * ny - 1)])
    sent(6, got_z.at[pl.ds(0, nz * sections - 1)])


def hand_on(sums, proofs, new_references, evidence, sems):
    copies = [
        pltpu.make_async_copy(sums, new_references, sems.at[0]),
        pltpu.make_async_copy(proofs, evidence, sems.at[1]),
    ]
    for copy in copies:
        copy.start()
    for copy in copies:
        copy.wait()


def body(
    dims,
    images,
    group_ids,
    row_filters,
    column_filters,
    basis_rows,
    basis_columns,
    rotations,
    references,
    sharpness,
    best_rotation,
    assignments,
):
    nz, nx, ny = dims
    sections = 4
    particles, pix = images.shape[0], images.shape[1]
    nb = basis_rows.shape[1]
    local, width = rotations.shape[0], rotations.shape[1]
    classes = 2 * nz * nx * ny
    wide = width + LANES
    bf16, f32 = jnp.bfloat16, jnp.float32
    hbm = pl.BlockSpec(memory_space=pltpu.HBM)
    vmem = pl.BlockSpec(memory_space=pltpu.VMEM)
    new_references, evidence = pl.pallas_call(
        functools.partial(kernel, dims),
        out_shape=(
            pltpu.VMEM((2, width), f32),
            pltpu.VMEM((1, particles), f32),
        ),
        in_specs=[hbm] * 12,
        out_specs=(vmem, vmem),
        scratch_shapes=[
            pltpu.VMEM((particles, pix, pix), bf16),
            pltpu.VMEM(row_filters.shape, bf16),
            pltpu.VMEM(column_filters.shape, bf16),
            pltpu.VMEM((pix, pix), f32),
            pltpu.VMEM(rotations.shape, bf16),
            pltpu.VMEM((2, nb, pix), bf16),
            pltpu.VMEM((pix, nb * nb), bf16),
            pltpu.VMEM((pix, nb * nb), f32),
            pltpu.SMEM((particles,), jnp.int32),
            pltpu.VMEM((2, width), bf16),
            pltpu.VMEM((1, particles), bf16),
            pltpu.VMEM((1, particles), jnp.int32),
            pltpu.VMEM(assignments.shape, jnp.int32),
            pltpu.VMEM((particles, nb * nb), f32),
            pltpu.VMEM((particles, pix), f32),
            pltpu.VMEM((ny, 2, width), bf16),
            pltpu.VMEM((nx * nz, 2 * ny, width), bf16),
            pltpu.VMEM((classes, classes), bf16),
            pltpu.VMEM((sections, particles, wide), bf16),
            pltpu.VMEM((local * sections * particles, width), bf16),
            pltpu.VMEM((sections, particles, width), bf16),
            pltpu.VMEM((sections, particles, width), bf16),
            pltpu.VMEM((sections, particles, classes), f32),
            pltpu.VMEM((sections, particles, classes), f32),
            pltpu.VMEM((nx * ny, 2 * nz, wide), bf16),
            pltpu.VMEM((nx * ny, 2 * nz, wide), bf16),
            pltpu.VMEM((nz, 2, wide), f32),
            pltpu.VMEM((nz * sections, 2, wide), f32),
            pltpu.SemaphoreType.DMA((particles,)),
            pltpu.SemaphoreType.DMA((11,)),
            pltpu.SemaphoreType.DMA((7,)),
            pltpu.SemaphoreType.DMA((7,)),
            pltpu.SemaphoreType.REGULAR,
        ],
        compiler_params=pltpu.CompilerParams(
            collective_id=0, has_side_effects=True, vmem_limit_bytes=63 * 1024 * 1024
        ),
    )(
        images,
        group_ids,
        row_filters,
        column_filters,
        basis_rows.T,
        basis_columns.T,
        jnp.asarray(soft_edge(pix)),
        rotations,
        references,
        sharpness.reshape(1, particles),
        best_rotation.reshape(1, particles),
        assignments,
    )
    new_references, evidence = pl.pallas_call(
        hand_on,
        out_shape=(
            jax.ShapeDtypeStruct((2, width), f32),
            jax.ShapeDtypeStruct((1, particles), f32),
        ),
        in_specs=[vmem, vmem],
        out_specs=(hbm, hbm),
        scratch_shapes=[pltpu.SemaphoreType.DMA((2,))],
        compiler_params=pltpu.CompilerParams(vmem_limit_bytes=1024 * 1024),
    )(new_references, evidence)
    return new_references, evidence.reshape(particles)


def solution(mesh, dims=TORUS):
    in_specs = (
        P(("section", "cls"), None, None),
        P(("section", "cls")),
        P(),
        P(),
        P(),
        P(),
        P("section", None, None),
        P("cls", None),
        P(("section", "cls")),
        P(("section", "cls")),
        P(("section", "cls"), None),
    )
    out_specs = (P("cls", None), P(("section", "cls")))
    return jax.shard_map(
        functools.partial(body, dims), mesh=mesh, in_specs=in_specs, out_specs=out_specs, check_vma=False
    )
```

```python
import functools
import math

import jax
import jax.numpy as jnp
import numpy as np
from jax import lax
from jax.experimental import pallas as pl
from jax.experimental.pallas import tpu as pltpu
from jax.sharding import PartitionSpec as P

EPSILON = 1e-05
TORUS = (4, 4, 8)
MESH = pl.DeviceIdType.MESH
LANES = 128


def soft_edge(pixels):
    coordinate = (np.arange(pixels, dtype=np.float32) - np.float32((pixels - 1) / 2.0)) / np.float32(pixels / 2.0)
    radius = np.sqrt(coordinate[:, None] * coordinate[:, None] + coordinate[None, :] * coordinate[None, :])
    falloff = np.clip((radius - np.float32(0.8)) / np.float32(0.15), 0.0, 1.0)
    return (0.5 + 0.5 * np.cos(math.pi * falloff)).astype(np.float32)


def contract_last(a, b):
    return lax.dot_general(a, b, (((1,), (1,)), ((), ())), preferred_element_type=jnp.float32)


def contract_first(a, b):
    return lax.dot_general(a, b, (((0,), (0,)), ((), ())), preferred_element_type=jnp.float32)


def kernel(
    dims,
    images,
    group_ids_hbm,
    row_filters,
    column_filters,
    basis_rows,
    basis_columns,
    mask,
    rotations,
    references_hbm,
    sharpness_hbm,
    best_rotation_hbm,
    assignments_hbm,
    new_references,
    evidence,
    img,
    rowf,
    colf,
    edge,
    rot,
    bas,
    tiled,
    spread,
    group_ids,
    references,
    sharpness,
    best_rotation,
    assignments,
    raw,
    squares,
    near,
    refs,
    reorder,
    coef,
    turned,
    turned_out,
    turned_in,
    marg_out,
    marg_in,
    sum_y,
    got_y,
    sum_z,
    got_z,
    img_sem,
    in_sem,
    send_sem,
    recv_sem,
    ready,
):
    nz, nx, ny = dims
    section, cls = lax.axis_index("section"), lax.axis_index("cls")
    sections = 4
    zh = cls // (nx * ny)
    xx = (cls // ny) % nx
    yy = cls % ny
    particles, pix = img.shape[0], img.shape[1]
    local = rot.shape[0]
    width = rot.shape[1]
    classes = nz * nx * ny * 2
    nb = bas.shape[1]

    def at(dz, dx, dy, ds):
        return {
            "section": (section + ds) % sections,
            "cls": (((zh + dz) % nz) * nx + (xx + dx) % nx) * ny + (yy + dy) % ny,
        }

    zl, core = section // 2, section % 2

    def above(dz, low):
        return {"section": low * 2 + core, "cls": (((zh + dz) % nz) * nx + xx) * ny + yy}

    along_y = sorted(range(1, ny), key=lambda d: -min(d, ny - d))
    along_x = sorted(range(1, nx), key=lambda d: -min(d, nx - d))
    along_z = sorted(range(nz), key=lambda d: -min(d, nz - d))
    inside = (2, 1, 3)
    peers = [at(0, 0, dy, 0) for dy in along_y]
    peers += [above(2, 1 - zl), above(1, 0), above(nz - 1, 1)]
    peers += [at(0, dx, 0, 0) for dx in along_x]
    peers += [at(0, 0, 0, ds) for ds in inside]
    barrier = pltpu.get_barrier_semaphore()
    for peer in peers:
        pl.semaphore_signal(barrier, inc=1, device_id=peer, device_id_type=MESH)

    inputs = {}
    for k, (src, dst) in enumerate(
        [
            (column_filters, colf),
            (row_filters, rowf),
            (basis_rows, bas.at[0]),
            (basis_columns, bas.at[1]),
            (mask, edge),
            (rotations, rot),
            (group_ids_hbm, group_ids),
            (references_hbm, references),
            (sharpness_hbm, sharpness),
            (best_rotation_hbm, best_rotation),
            (assignments_hbm, assignments),
        ]
    ):
        inputs[k] = pltpu.make_async_copy(src, dst, in_sem.at[k])
    for k in (2, 3, 6, 0):
        inputs[k].start()
    pltpu.make_async_copy(images.at[0], img.at[0], img_sem.at[0]).start()
    for k in (1, 4, 7):
        inputs[k].start()

    @pl.loop(1, particles)
    def _(n):
        pltpu.make_async_copy(images.at[n], img.at[n], img_sem.at[n]).start()

    for k in (8, 9, 10):
        inputs[k].start()
    inputs[5].start()

    inputs[2].wait()
    inputs[3].wait()
    row_at = lax.broadcasted_iota(jnp.int32, (nb, nb * nb), 0)
    lane_at = lax.broadcasted_iota(jnp.int32, (nb, nb * nb), 1)
    minor = (lane_at % nb == row_at).astype(jnp.float32).astype(jnp.bfloat16)
    major = (lane_at // nb == row_at).astype(jnp.float32).astype(jnp.bfloat16)
    tiled[...] = contract_first(bas[1], minor).astype(jnp.bfloat16)
    spread[...] = contract_first(bas[0], major)
    inputs[0].wait()
    inputs[1].wait()
    inputs[4].wait()
    inputs[6].wait()

    def filter_images(low, high, together):
        @pl.loop(low, high, step=together)
        def _(n):
            some = [n + k for k in range(together)]
            halves = []
            for m in some:
                pltpu.make_async_copy(images.at[m], img.at[m], img_sem.at[m]).wait()
                half = jnp.dot(img[m], colf[group_ids[m]], preferred_element_type=jnp.float32)
                halves.append(half.astype(jnp.bfloat16))
            masked = [
                jnp.dot(rowf[group_ids[m]], half, preferred_element_type=jnp.float32) * edge[...]
                for m, half in zip(some, halves)
            ]
            for m, one in zip(some, masked):
                squares[pl.ds(m, 1), :] = jnp.sum(one * one, axis=0, keepdims=True)
            inner = [jnp.dot(one.astype(jnp.bfloat16), tiled[...], preferred_element_type=jnp.float32) for one in masked]
            for m, one in zip(some, inner):
                raw[pl.ds(m, 1), :] = jnp.sum(one * spread[...], axis=0, keepdims=True)

    def send(k, src, dst, to):
        pltpu.make_async_remote_copy(
            src_ref=src,
            dst_ref=dst,
            send_sem=send_sem.at[k],
            recv_sem=recv_sem.at[k],
            device_id=to,
            device_id_type=MESH,
        ).start()

    def arrived(k, ref):
        pltpu.make_async_copy(ref, ref, recv_sem.at[k]).wait()

    def sent(k, ref):
        pltpu.make_async_copy(ref, ref, send_sem.at[k]).wait()

    filter_images(0, particles // 4, 4)

    pl.semaphore_wait(barrier, len(peers))
    inputs[7].wait()
    near[0] = references[...]
    for dy in along_y:
        send(0, near.at[0], near.at[ny - dy], at(0, 0, dy, 0))
    for dx in along_x:
        pl.semaphore_signal(ready, inc=1, device_id=at(0, dx, 0, 0), device_id_type=MESH)
    filter_images(particles // 4, particles, 6)

    eye = lax.broadcasted_iota(jnp.int32, (particles, particles), 0) == lax.broadcasted_iota(
        jnp.int32, (particles, particles), 1
    )
    inputs[8].wait()
    inputs[9].wait()
    sharp_row = sharpness[...].astype(jnp.float32)
    sharp = jnp.sum(jnp.where(eye, jnp.broadcast_to(sharp_row, (particles, particles)), 0.0), axis=1, keepdims=True)
    best_row = best_rotation[...].astype(jnp.float32)
    best = jnp.sum(jnp.where(eye, jnp.broadcast_to(best_row, (particles, particles)), 0.0), axis=1, keepdims=True)
    power = jnp.sum(squares[...], axis=1, keepdims=True) * (1.0 / (pix * pix))
    scale = lax.rsqrt(power + EPSILON) * sharp
    coef[0, :, 0:width] = (raw[...] * scale).astype(jnp.bfloat16)
    coef[0, :, width:] = jnp.broadcast_to(best, (particles, LANES)).astype(jnp.bfloat16)
    for ds in inside:
        send(2, coef.at[0], coef.at[sections - ds], at(0, 0, 0, ds))

    arrived(0, near.at[pl.ds(1, ny - 1)])
    refs[0] = jnp.concatenate([near[dy].astype(jnp.float32) for dy in range(ny)], axis=0).astype(jnp.bfloat16)
    pl.semaphore_wait(ready, nx - 1)
    side = 1 + (nz - 2) * zl
    for dx in (2, 1, 3, 0):
        if dx >= nx:
            continue
        for dz, low, slot in ((2, 1 - zl, 2), (2 * zl - 1 + nz, zl, side), (2 * zl - 1 + nz, 1 - zl, side), (0, zl, 0)):
            if dx or not isinstance(dz, int) or dz:
                to = {"section": low * 2 + core, "cls": (((zh + dz) % nz) * nx + (xx + dx) % nx) * ny + yy}
                send(1, refs.at[0], refs.at[(nx - dx) % nx * nz + slot], to)

    place = lax.broadcasted_iota(jnp.int32, (particles, classes), 1)
    dx_at, rest = place // (nz * ny * 2), place % (nz * ny * 2)
    dz_at, rest = rest // (ny * 2), rest % (ny * 2)
    dy_at, last = rest // 2, rest % 2
    name = ((((zh + dz_at) % nz) * nx + (xx + dx_at) % nx) * ny + (yy + dy_at) % ny) * 2 + last
    inputs[10].wait()
    listed = jnp.zeros((particles, classes), jnp.float32)
    for j in range(assignments.shape[1]):
        listed = jnp.where(assignments[:, j : j + 1] == name, 1.0, listed)

    place = lax.broadcasted_iota(jnp.int32, (classes, classes), 1)
    dx_at, rest = place // (ny * nz * 2), place % (ny * nz * 2)
    dy_at, rest = rest // (nz * 2), rest % (nz * 2)
    place = dx_at * (nz * ny * 2) + (rest // 2) * (ny * 2) + dy_at * 2 + rest % 2
    place = place == lax.broadcasted_iota(jnp.int32, (classes, classes), 0)
    reorder[...] = jnp.where(place, 1.0, 0.0).astype(jnp.bfloat16)

    inputs[5].wait()
    arrived(2, coef.at[pl.ds(1, sections - 1)])
    everyone = sections * particles
    gathered = coef[:, :, 0:width].reshape(everyone, width)
    best_all = coef[:, :, width:].astype(jnp.float32).reshape(everyone, LANES)
    best_all = jnp.concatenate([best_all] * (width // LANES), axis=1)
    first = (section * local).astype(jnp.float32)
    aligned = jnp.zeros((everyone, width), jnp.float32)
    for r in range(local):
        one = contract_last(gathered, rot[r])
        aligned = jnp.where(best_all == first + float(r), one, aligned)
        turned[pl.ds(r * everyone, everyone), :] = one.astype(jnp.bfloat16)
    turned_out[...] = aligned.astype(jnp.bfloat16).reshape(sections, particles, width)
    for ds in inside:
        send(3, turned_out.at[ds], turned_in.at[sections - ds], at(0, 0, 0, ds))

    arrived(3, turned_in.at[pl.ds(1, sections - 1)])
    mine = functools.reduce(
        jnp.add, [turned_out[0].astype(jnp.float32)] + [turned_in[d].astype(jnp.float32) for d in range(1, sections)]
    )
    mine = (mine * (1.0 / sharp)).astype(jnp.bfloat16)
    with_one = jnp.concatenate([mine, jnp.ones((particles, LANES), jnp.bfloat16)], axis=1)

    arrived(1, refs.at[pl.ds(1, nx * nz - 1)])
    all_refs = refs[...].reshape(classes, width)
    scores = contract_last(turned[...], all_refs).reshape(local, everyone, classes)
    largest = jnp.max(scores, axis=0)
    total = jnp.sum(jnp.exp(scores - largest), axis=0)
    marg_out[...] = (largest + jnp.log(total)).reshape(sections, particles, classes)
    for ds in inside:
        send(4, marg_out.at[ds], marg_in.at[sections - ds], at(0, 0, 0, ds))
    order = [(dx, dy) for dx in range(nx) for dy in range(ny) if (dx, dy) != (0, 0)]
    order = sorted(order, key=lambda d: -min(d[0], nx - d[0]) - min(d[1], ny - d[1]))
    owners = [at(0, dx, dy, 0) for dx, dy in order]
    arrived(4, marg_in.at[pl.ds(1, sections - 1)])
    parts = [marg_out[0]] + [marg_in[d] for d in range(1, sections)]
    largest = functools.reduce(jnp.maximum, parts)
    marg = largest + jnp.log(functools.reduce(jnp.add, [jnp.exp(one - largest) for one in parts]))
    highest = jnp.max(jnp.where(listed > 0.0, marg, -jnp.inf), axis=1, keepdims=True)
    weight = jnp.where(listed > 0.0, jnp.exp(marg - highest), 0.0)
    weight = (weight / jnp.sum(weight, axis=1, keepdims=True)).astype(jnp.bfloat16)
    weight = jnp.dot(weight, reorder[...], preferred_element_type=jnp.float32).astype(jnp.bfloat16)
    sums = contract_first(weight, with_one)
    sum_y[...] = sums.reshape(sum_y.shape).astype(jnp.bfloat16)
    for (dx, dy), owner in zip(order, owners):
        send(5, sum_y.at[dx * ny + dy], got_y.at[dx * ny + dy], owner)

    peak = jnp.max(marg, axis=1, keepdims=True)
    proof = peak + jnp.log(jnp.sum(jnp.exp(marg - peak), axis=1, keepdims=True))
    evidence[...] = jnp.sum(jnp.where(eye, jnp.broadcast_to(proof, (particles, particles)), 0.0), axis=0, keepdims=True)

    arrived(5, got_y.at[pl.ds(1, nx * ny - 1)])
    total = functools.reduce(
        jnp.add, [sum_y[0].astype(jnp.float32)] + [got_y[d].astype(jnp.float32) for d in range(1, nx * ny)]
    )
    for dz in range(nz):
        sum_z[dz] = total[2 * dz : 2 * dz + 2]
    for dz in along_z:
        for ds in (*inside, 0):
            if (dz, ds) != (0, 0):
                send(6, sum_z.at[dz], got_z.at[dz * sections + section], at(dz, 0, 0, ds))
    got_z[section] = sum_z[0]
    arrived(6, got_z.at[pl.ds(0, nz * sections - 1)])
    total = functools.reduce(jnp.add, [got_z[d] for d in range(nz * sections)])
    over = total[:, width:] + 1.0
    over = jnp.concatenate([over] * (width // LANES), axis=1)
    new_references[...] = (total[:, 0:width] + references[...].astype(jnp.float32)) / over

    sent(0, near.at[pl.ds(1, ny - 1)])
    sent(1, refs.at[pl.ds(1, nx * nz - 1)])
    sent(2, coef.at[pl.ds(1, sections - 1)])
    sent(3, turned_out.at[pl.ds(1, sections - 1)])
    sent(4, marg_out.at[pl.ds(1, sections - 1)])
    sent(5, sum_y.at[pl.ds(1, nx * ny - 1)])
    sent(6, got_z.at[pl.ds(0, nz * sections - 1)])


def hand_on(sums, proofs, new_references, evidence, sems):
    copies = [
        pltpu.make_async_copy(sums, new_references, sems.at[0]),
        pltpu.make_async_copy(proofs, evidence, sems.at[1]),
    ]
    for copy in copies:
        copy.start()
    for copy in copies:
        copy.wait()


def body(
    dims,
    images,
    group_ids,
    row_filters,
    column_filters,
    basis_rows,
    basis_columns,
    rotations,
    references,
    sharpness,
    best_rotation,
    assignments,
):
    nz, nx, ny = dims
    sections = 4
    particles, pix = images.shape[0], images.shape[1]
    nb = basis_rows.shape[1]
    local, width = rotations.shape[0], rotations.shape[1]
    classes = 2 * nz * nx * ny
    wide = width + LANES
    bf16, f32 = jnp.bfloat16, jnp.float32
    hbm = pl.BlockSpec(memory_space=pltpu.HBM)
    vmem = pl.BlockSpec(memory_space=pltpu.VMEM)
    new_references, evidence = pl.pallas_call(
        functools.partial(kernel, dims),
        out_shape=(
            pltpu.VMEM((2, width), f32),
            pltpu.VMEM((1, particles), f32),
        ),
        in_specs=[hbm] * 12,
        out_specs=(vmem, vmem),
        scratch_shapes=[
            pltpu.VMEM((particles, pix, pix), bf16),
            pltpu.VMEM(row_filters.shape, bf16),
            pltpu.VMEM(column_filters.shape, bf16),
            pltpu.VMEM((pix, pix), f32),
            pltpu.VMEM(rotations.shape, bf16),
            pltpu.VMEM((2, nb, pix), bf16),
            pltpu.VMEM((pix, nb * nb), bf16),
            pltpu.VMEM((pix, nb * nb), f32),
            pltpu.SMEM((particles,), jnp.int32),
            pltpu.VMEM((2, width), bf16),
            pltpu.VMEM((1, particles), bf16),
            pltpu.VMEM((1, particles), jnp.int32),
            pltpu.VMEM(assignments.shape, jnp.int32),
            pltpu.VMEM((particles, nb * nb), f32),
            pltpu.VMEM((particles, pix), f32),
            pltpu.VMEM((ny, 2, width), bf16),
            pltpu.VMEM((nx * nz, 2 * ny, width), bf16),
            pltpu.VMEM((classes, classes), bf16),
            pltpu.VMEM((sections, particles, wide), bf16),
            pltpu.VMEM((local * sections * particles, width), bf16),
            pltpu.VMEM((sections, particles, width), bf16),
            pltpu.VMEM((sections, particles, width), bf16),
            pltpu.VMEM((sections, particles, classes), f32),
            pltpu.VMEM((sections, particles, classes), f32),
            pltpu.VMEM((nx * ny, 2 * nz, wide), bf16),
            pltpu.VMEM((nx * ny, 2 * nz, wide), bf16),
            pltpu.VMEM((nz, 2, wide), f32),
            pltpu.VMEM((nz * sections, 2, wide), f32),
            pltpu.SemaphoreType.DMA((particles,)),
            pltpu.SemaphoreType.DMA((11,)),
            pltpu.SemaphoreType.DMA((7,)),
            pltpu.SemaphoreType.DMA((7,)),
            pltpu.SemaphoreType.REGULAR,
        ],
        compiler_params=pltpu.CompilerParams(
            collective_id=0, has_side_effects=True, vmem_limit_bytes=63 * 1024 * 1024
        ),
    )(
        images,
        group_ids,
        row_filters,
        column_filters,
        basis_rows.T,
        basis_columns.T,
        jnp.asarray(soft_edge(pix)),
        rotations,
        references,
        sharpness.reshape(1, particles),
        best_rotation.reshape(1, particles),
        assignments,
    )
    new_references, evidence = pl.pallas_call(
        hand_on,
        out_shape=(
            jax.ShapeDtypeStruct((2, width), f32),
            jax.ShapeDtypeStruct((1, particles), f32),
        ),
        in_specs=[vmem, vmem],
        out_specs=(hbm, hbm),
        scratch_shapes=[pltpu.SemaphoreType.DMA((2,))],
        compiler_params=pltpu.CompilerParams(vmem_limit_bytes=1024 * 1024),
    )(new_references, evidence)
    return new_references, evidence.reshape(particles)


def solution(mesh, dims=TORUS):
    in_specs = (
        P(("section", "cls"), None, None),
        P(("section", "cls")),
        P(),
        P(),
        P(),
        P(),
        P("section", None, None),
        P("cls", None),
        P(("section", "cls")),
        P(("section", "cls")),
        P(("section", "cls"), None),
    )
    out_specs = (P("cls", None), P(("section", "cls")))
    return jax.shard_map(
        functools.partial(body, dims), mesh=mesh, in_specs=in_specs, out_specs=out_specs, check_vma=False
    )
```
